768 devices in a mesh: lon: 48 (over y_hi, z), lat: 16 (over x, y_lo, core).
Axes of the slice: x: 4, y: 8 (y_hi: 4, y_lo: 2; y = y_hi * 2 + y_lo), z: 12, core: 2. Of those that a mesh axis runs over, the one named last changes fastest.
Arguments:
- tracers: float32 [4, 8, 256, 6144], P(None, None, 'lat', 'lon'), may hold values from -6 to 6
- east_speed: float32 [8, 256, 6144], P(None, 'lat', 'lon'), may hold values from -1.25 to 1.25
- north_speed: float32 [8, 256, 6144], P(None, 'lat', 'lon'), may hold values from -1.25 to 1.25
- mixing_coef: float32 [7, 256, 6144], P(None, 'lat', 'lon'), may hold values from 0.05 to 5
- ocean_mask: int32 [256, 6144], P('lat', 'lon'), may hold values 0 or 1
- fold_map: int32 [6144], P('lon'), may hold values from 0 to 6143, as said below
- atmos_state: float32 [4, 786432], P(None, ('lon', 'lat')), may hold values from -6 to 6
- atmos_coef: float32 [786432], P(('lon', 'lat')), may hold values from 0.1 to 1
- xgrid_cell: int32 [4718592], P(('lon', 'lat')), may hold values from 0 to 2047
- xgrid_atm: int32 [4718592], P(('lon', 'lat')), may hold values from 0 to 1023
- xgrid_owner: int32 [4718592, 1], P(('lon', 'lat')), may hold values from 0 to 47; in each aligned block of 6144 rows (0 to 6143, 6144 to 12287, ...) at most 256 rows name the same one
- xgrid_weight: float32 [4718592], P(('lon', 'lat')), may hold values from 0.2 to 1
Outputs:
- tracers_next: float32 [4, 8, 256, 6144], P(None, None, 'lat', 'lon')
The draws below stay inside these ranges and needn't reach their ends.
Inputs may be any that keep to these rules, and one draw needn't show every extreme that they name: `fold_map`: the mirror longitude of each top-row point; applying it twice gives the identity, and no point is its own mirror. `xgrid_cell`: row * 128 + column of the ocean cell inside the tile that holds the list row. `xgrid_atm`: atmosphere cell inside the owner's block. `xgrid_owner`: longitude tile of the atmosphere owner, in the list row's latitude row; within the rows of one tile no owner appears more than 256 times. `ocean_mask`: 1 for ocean, 0 for land.
All inputs are finite; a program needn't handle non-finite values. No bound on the sum of `ocean_mask` on one device may be relied on, other than what follows from the above.
Results may differ from the reference program's by a relative error of at most 0.0003.
Values sent between devices are 32-bit elements; how exact they have to be, the bound alone decides.
A program may use at most 128 MiB of HBM per device.

```python
import math
import jax
import jax.numpy as jnp
import numpy as np

TRACERS = 4
LEVELS = 8
CLAT = 16
CLON = 128
XR = 6144
ATM_DEV = 1024
NLAT = 256
NLON = 6144
CAP = 256
XROWS = 4718592
ATMS = 786432
N_LON = 48
N_LAT = 16


def draw_fold_map(key, part):
    shuffled = jax.random.permutation(key, NLON).astype(jnp.int32)
    partner = shuffled.reshape(NLON // 2, 2)[:, ::-1].reshape(NLON)
    return jnp.zeros((NLON,), jnp.int32).at[shuffled].set(partner).astype(jnp.int32)


def set_ends(array, own_key, low, top_value):
    longest = array.shape.index(max(array.shape))
    spots = []
    for shift in (0, 1):
        where = [jax.random.randint(jax.random.fold_in(own_key, axis), (), 0, length) for axis, length in enumerate(array.shape)]
        where[longest] = (where[longest] + shift) % array.shape[longest]
        spots.append(tuple(where))
    return array.at[spots[0]].set(low).at[spots[1]].set(top_value)


def steps_of(own_key, shape, cuts, smallest, top_value):
    level, own = 1.0, jax.random.fold_in(own_key, 6)
    for position, parts in cuts:
        draws = jnp.exp(jax.random.uniform(jax.random.fold_in(own, position), (parts,), jnp.float32, smallest / len(cuts), top_value / len(cuts)))
        level = level * jnp.repeat(draws, shape[position] // parts).reshape([-1 if axis == position else 1 for axis in range(len(shape))])
    return level


def shared_out(stream_key, own, number, rows, number_of, top, reach, skew):
    sequence = jax.random.permutation(stream_key, number_of)
    heavy_load, common = portions_of(number_of, rows * top, reach, skew, True), portions_of(number_of, rows * top, reach, skew, False)
    places = jnp.arange(number_of)

    def named(lengths, rotation):
        used = int((lengths > 0).sum())
        fixed = max(1, used // 4)
        shifted = fixed + (places - fixed + rotation * (used - fixed)) % max(1, number_of - fixed)
        return jnp.zeros((number_of,), jnp.int32).at[sequence[jnp.where(places < fixed, places, shifted)]].set(jnp.asarray(lengths, jnp.int32))

    lengths = jnp.where(number % 4 == 0, named(heavy_load, number // 4), named(common, number - number // 4 - 1))
    mixed = jax.random.permutation(jax.random.fold_in(own, 3), number_of)
    donor, receiver = mixed[0:number_of // 2 * 2:2], mixed[1:number_of // 2 * 2:2]
    room = jnp.minimum(lengths[donor] - 1, reach - lengths[receiver]) // 2
    room = jnp.where((donor == sequence[0]) | (receiver == sequence[0]) | (lengths[receiver] == 0), 0, jnp.maximum(room, 0))
    shifted = jax.random.randint(jax.random.fold_in(own, 4), (number_of // 2,), 0, 1 << 20) % (room + 1)
    lengths = lengths.at[donor].add(-shifted).at[receiver].add(shifted)
    labels = jnp.searchsorted(jnp.cumsum(lengths), jnp.arange(rows * top), side="right").astype(jnp.int32)
    table = labels.reshape(top, rows).T
    table = table[jax.random.permutation(jax.random.fold_in(own, 1), rows)]
    rotation = jax.random.randint(jax.random.fold_in(own, 2), (rows, 1), 0, top)
    return jnp.take_along_axis(table, (jnp.arange(top)[None, :] + rotation) % top, axis=1)


def portions_of(number_of, total, reach, slope, full):
    portions = [(1 << 20) // math.isqrt(grade ** slope) + 1 for grade in range(1, number_of + 1)]
    largest = reach if full else min(reach, max(-(-total // number_of), total * portions[0] // sum(portions)))
    least = 1 if total - largest >= number_of - 1 else 0
    holding, rest = [largest] + [least] * (number_of - 1), total - largest - least * (number_of - 1)
    while rest > 0:
        candidates = [i for i in range(1, number_of) if holding[i] < largest] or [i for i in range(1, number_of) if holding[i] < reach]
        mass, budget = sum([portions[i] for i in candidates]), rest
        for i in candidates:
            addition = min(reach - holding[i], max(1, budget * portions[i] // mass), rest)
            holding[i] = holding[i] + addition
            rest = rest - addition
    return np.array(holding)


def bell_draw(key, extent, width, bound, shards=(), kind=jnp.bfloat16):
    entries = width * jax.random.normal(key, extent, jnp.float32)
    if shards:
        entries = entries * steps_of(key, extent, shards, -0.22, 0.18)
    return jnp.clip(entries, -bound, bound).astype(kind)


def setup_inputs(seed: int = 0) -> dict:
    key_list = jax.random.split(jax.random.key(seed), 13)
    tracers = bell_draw(key_list[0], (TRACERS, LEVELS, NLAT, NLON), 1.0, 6.0, ((2, 16), (3, 48)), jnp.float32)
    east_speed = bell_draw(key_list[1], (LEVELS, NLAT, NLON), 0.08, 1.25, ((1, 16), (2, 48)), jnp.float32)
    north_speed = bell_draw(key_list[2], (LEVELS, NLAT, NLON), 0.08, 1.25, ((1, 16), (2, 48)), jnp.float32)
    mixing_coef = jnp.clip(jnp.exp(math.log(5.0) - 4.6051702 * jax.random.uniform(key_list[3], (LEVELS - 1, NLAT, NLON), jnp.float32) ** steps_of(key_list[3], (LEVELS - 1, NLAT, NLON), ((1, 16), (2, 48)), -0.2, 0.2)), 0.05, 5.0)
    ocean_mask = set_ends((jax.random.randint(key_list[4], (NLAT, NLON), 0, 4) < 3).astype(jnp.int32), jax.random.fold_in(key_list[4], 1), 0, 1)
    fold_map = draw_fold_map(jax.random.fold_in(key_list[12], 71), 0)
    atmos_state = bell_draw(key_list[6], (TRACERS, ATMS), 1.0, 6.0, ((1, 768),), jnp.float32)
    atmos_coef = jnp.clip(jnp.exp(math.log(1.0) - 2.3025851 * jax.random.uniform(key_list[7], (ATMS,), jnp.float32) ** steps_of(key_list[7], (ATMS,), ((0, 768),), -0.2, 0.2)), 0.1, 1.0)
    xgrid_cell = set_ends(jax.random.randint(key_list[8], (XROWS,), 0, CLAT * CLON), jax.random.fold_in(key_list[8], 1), 0, (CLAT * CLON) - 1).astype(jnp.int32)
    xgrid_atm = set_ends(jax.random.randint(key_list[9], (XROWS,), 0, ATM_DEV), jax.random.fold_in(key_list[9], 1), 0, ATM_DEV - 1).astype(jnp.int32)
    xgrid_owner_keys = jax.random.split(jax.random.fold_in(key_list[10], 1), XROWS // XR)
    xgrid_owner_turns = jax.random.permutation(jax.random.fold_in(key_list[10], 3), XROWS // XR)
    xgrid_owner = jax.vmap(lambda own, number: shared_out(jax.random.fold_in(key_list[10], 2), own, number, XR, N_LON, 1, CAP, 2))(xgrid_owner_keys, xgrid_owner_turns).reshape((XROWS, 1))
    xgrid_weight = jnp.clip(0.2 + 0.8 * jax.random.uniform(key_list[11], (XROWS,), jnp.float32) ** steps_of(key_list[11], (XROWS,), ((0, 768),), -0.2, 0.2), 0.2, 1.0)
    return {"tracers": tracers, "east_speed": east_speed, "north_speed": north_speed, "mixing_coef": mixing_coef, "ocean_mask": ocean_mask, "fold_map": fold_map, "atmos_state": atmos_state, "atmos_coef": atmos_coef, "xgrid_cell": xgrid_cell, "xgrid_atm": xgrid_atm, "xgrid_owner": xgrid_owner, "xgrid_weight": xgrid_weight}


flux_step = 0.5


def solve_columns(right_side, mixing_coef):
    levels = right_side.shape[-3]
    zero_plane = jnp.zeros_like(mixing_coef[0])
    ratios = []
    values = []
    for level in range(levels):
        upper_coef = mixing_coef[level - 1] if level > 0 else zero_plane
        lower_coef = mixing_coef[level] if level < levels - 1 else zero_plane
        diagonal = 1.0 + upper_coef + lower_coef
        if level == 0:
            pivot_value = diagonal
            value = right_side[..., 0, :, :] / pivot_value
        else:
            pivot_value = diagonal - upper_coef * ratios[-1]
            value = (right_side[..., level, :, :] + upper_coef * values[-1]) / pivot_value
        ratios.append(lower_coef / pivot_value)
        values.append(value)
    result = [values[-1]]
    for level in range(levels - 2, -1, -1):
        result.append(values[level] + ratios[level] * result[-1])
    return jnp.stack(result[::-1], axis=-3)


def reference(tracers, east_speed, north_speed, mixing_coef, ocean_mask, fold_map, atmos_state, atmos_coef, xgrid_cell, xgrid_atm, xgrid_owner, xgrid_weight):
    mask = ocean_mask.astype(jnp.float32)
    mask_east = jnp.roll(mask, -1, axis=1)
    mask_north = jnp.concatenate([mask[1:], mask[NLAT - 1:][:, fold_map]], axis=0)
    block_ids = jnp.arange(XROWS, dtype=jnp.int32) // XR
    lon_tile = block_ids // N_LAT
    lat_tile = block_ids % N_LAT
    grid_row = lat_tile * CLAT + xgrid_cell // CLON
    grid_col = lon_tile * CLON + xgrid_cell % CLON
    grid_cell = grid_row * NLON + grid_col
    surface = tracers[:, 0].reshape(TRACERS, NLAT * NLON)
    ocean_side = jnp.take(surface, grid_cell, axis=1)
    atm_global = (xgrid_owner[:, 0] * N_LAT + lat_tile) * ATM_DEV + xgrid_atm
    row_flux = jnp.take(atmos_coef, atm_global)[None] * (jnp.take(atmos_state, atm_global, axis=1) - ocean_side)
    contrib = xgrid_weight[None] * row_flux
    surface_sum = jax.ops.segment_sum(contrib.T, grid_cell, num_segments=NLAT * NLON).T.reshape(TRACERS, NLAT, NLON)
    outputs = []
    for tracer in range(TRACERS):
        field = tracers[tracer]
        east_cell = jnp.roll(field, -1, axis=2)
        flux_east = east_speed * jnp.where(east_speed > 0, field, east_cell) * (mask * mask_east)
        flux_west = jnp.roll(flux_east, 1, axis=2)
        north_cell = jnp.concatenate([field[:, 1:], field[:, NLAT - 1:][:, :, fold_map]], axis=1)
        flux_north = north_speed * jnp.where(north_speed > 0, field, north_cell) * (mask * mask_north)
        flux_south = jnp.concatenate([jnp.zeros_like(flux_north[:, :1]), flux_north[:, :-1]], axis=1)
        advected = field - (flux_east - flux_west + flux_north - flux_south)
        forced = advected.at[0].set(advected[0] + flux_step * surface_sum[tracer])
        outputs.append(solve_columns(forced, mixing_coef) * mask)
    return jnp.stack(outputs, axis=0)
```

```python
import jax
import jax.numpy as jnp
from jax import lax
from jax.experimental import pallas as pl
from jax.experimental.pallas import tpu as pltpu
from jax.sharding import PartitionSpec as P

flux_step = 0.5
LANES = 128
WIDE = 512


def pack_kernel(tr, es, ns, om, state, coef, gat, north, south, east, west):
    tracer_count, level_count, row_count, cols = tr.shape
    blocks = state.shape[1] // LANES
    for t in range(tracer_count):
        for h in range(blocks):
            gat[t * blocks + h : t * blocks + h + 1, :] = state[t : t + 1, h * LANES : (h + 1) * LANES]
    gat[tracer_count * blocks : (tracer_count + 1) * blocks, :] = coef[...]
    base = (tracer_count + 1) * blocks
    plane_count = tracer_count * level_count
    lane = lax.broadcasted_iota(jnp.int32, (row_count, cols), 1)
    mask = om[...].astype(jnp.float32)
    gat[base:, :] = jnp.zeros((gat.shape[0] - base, cols), jnp.float32)
    north[...] = jnp.zeros_like(north)
    south[...] = jnp.zeros_like(south)
    first = jnp.zeros((row_count, cols), jnp.float32)
    last = jnp.zeros((row_count, cols), jnp.float32)
    for p in range(plane_count + 1 + level_count):
        if p < plane_count:
            plane = tr[p // level_count, p % level_count]
            north_plane = plane
        elif p == plane_count:
            plane = mask
            north_plane = plane
        else:
            plane = es[p - plane_count - 1]
            north_plane = ns[p - plane_count - 1]
        north[p : p + 1, :] = north_plane[row_count - 1 : row_count, :]
        last = jnp.where(lane == p, plane[:, cols - 1 : cols], last)
        if p <= plane_count:
            gat[base + p : base + p + 1, :] = plane[row_count - 1 : row_count, :]
            south[p : p + 1, :] = plane[0:1, :]
            first = jnp.where(lane == p, plane[:, 0:1], first)
    east[...] = last
    west[...] = first


def split(x, pieces):
    out = []
    for i in range(pieces):
        top = x.astype(jnp.bfloat16)
        out.append(top)
        x = x - top.astype(jnp.float32)
    return out


def main_kernel(
    tr, es, ns, mix, om, fold, gat, from_south, from_north, from_west, from_east,
    cell, atm, owner, weight, out, table, total, mirror,
):
    tracer_count, level_count, row_count, cols = tr.shape
    lon_count = gat.shape[0]
    values = tracer_count + 1
    blocks = 1024 // LANES
    base = values * blocks
    hi_count = lon_count * blocks
    plane_count = tracer_count * level_count
    lat_count = lax.axis_size("lat")
    is_top = lax.axis_index("lat") == lat_count - 1

    coef = gat[:, tracer_count * blocks : base, :].reshape(hi_count, LANES)
    for t in range(values):
        if t < tracer_count:
            block = gat[:, t * blocks : (t + 1) * blocks, :].reshape(hi_count, LANES) * coef
        else:
            block = coef
        turned = block.T
        for i, piece in enumerate(split(turned, 2)):
            table[t * LANES : (t + 1) * LANES, i * hi_count : (i + 1) * hi_count] = piece

    total[...] = jnp.zeros_like(total)
    rows_each = WIDE // LANES

    def step(k, carry):
        def rows(ref):
            return jnp.concatenate(
                [ref[pl.ds(k * rows_each + i, 1), :] for i in range(rows_each)], axis=1
            )

        cells, atms, owners, weights = rows(cell), rows(atm), rows(owner), rows(weight)
        hi = owners * blocks + (atms >> 7)
        lo = atms & (LANES - 1)
        hi_hot = (lax.broadcasted_iota(jnp.int32, (hi_count, WIDE), 0) == hi).astype(
            jnp.float32
        ).astype(jnp.bfloat16)
        picked = jnp.dot(
            table[...], jnp.concatenate([hi_hot, hi_hot], axis=0),
            preferred_element_type=jnp.float32,
        )
        lane_row = lax.broadcasted_iota(jnp.int32, (LANES, WIDE), 0)
        lo_mask = lane_row == lo
        col_hot = (lane_row == (cells & (cols - 1))).astype(jnp.float32).astype(jnp.bfloat16)
        row_mask = lax.broadcasted_iota(jnp.int32, (row_count, WIDE), 0) == (cells >> 7)
        parts = []
        for t in range(values):
            chosen = jnp.where(lo_mask, picked[t * LANES : (t + 1) * LANES, :], 0.0)
            value = jnp.sum(chosen, axis=0, keepdims=True) * weights
            parts.append(jnp.where(row_mask, value, 0.0))
        left = jnp.concatenate(parts, axis=0)
        left = jnp.concatenate(split(left, 2), axis=0)
        total[...] += lax.dot_general(
            left, col_hot, (((1,), (1,)), ((), ())), preferred_element_type=jnp.float32
        )
        return carry

    lax.fori_loop(0, cell.shape[0] // rows_each, step, 0)

    mirror[...] = from_north[...]

    @pl.when(is_top)
    def _():
        lane_row = lax.broadcasted_iota(jnp.int32, (2 * LANES, LANES), 0)
        pad = mirror.shape[0]

        def fold_step(k, acc):
            both = jnp.concatenate(
                [gat[2 * k, base : base + pad, :], gat[2 * k + 1, base : base + pad, :]], axis=1
            )
            hot = (lane_row == fold[...] - k * (2 * LANES)).astype(jnp.float32).astype(jnp.bfloat16)
            return acc + jnp.dot(
                jnp.concatenate(split(both, 3), axis=0), hot, preferred_element_type=jnp.float32
            )

        acc = lax.fori_loop(
            0, lon_count // 2, fold_step, jnp.zeros((3 * pad, LANES), jnp.float32)
        )
        mirror[...] = acc[:pad] + acc[pad : 2 * pad] + acc[2 * pad :]

    mask = om[...].astype(jnp.float32)
    lane = lax.broadcasted_iota(jnp.int32, (row_count, cols), 1)
    row = lax.broadcasted_iota(jnp.int32, (row_count, cols), 0)
    west_cols = from_west[...]
    east_cols = from_east[...]

    def to_west(x, p):
        return jnp.where(lane == 0, west_cols[:, p : p + 1], pltpu.roll(x, 1, 1))

    def to_east(x, p):
        return jnp.where(lane == cols - 1, east_cols[:, p : p + 1], pltpu.roll(x, cols - 1, 1))

    def to_south(x, p):
        return jnp.where(row == 0, from_south[p : p + 1, :], pltpu.roll(x, 1, 0))

    def to_north(x, p):
        return jnp.where(row == row_count - 1, mirror[p : p + 1, :], pltpu.roll(x, row_count - 1, 0))

    mask_at = plane_count
    open_east = mask * to_east(mask, mask_at)
    open_west = to_west(mask, mask_at) * mask
    open_north = mask * to_north(mask, mask_at)
    open_south = to_south(mask, mask_at) * mask
    pivots = []
    ratios = []
    for level in range(level_count):
        lower = mix[level] if level < level_count - 1 else jnp.zeros_like(mask)
        if level == 0:
            pivot = 1.0 + lower
        else:
            pivot = 1.0 + mix[level - 1] + lower - mix[level - 1] * ratios[-1]
        inverse = 1.0 / pivot
        pivots.append(inverse)
        ratios.append(lower * inverse)
    done = [[] for _ in range(tracer_count)]
    lines = tracer_count + 1
    half = lines * row_count
    sums = total[0:half, :] + total[half : 2 * half, :]
    last_sum = sums[tracer_count * row_count :, :]
    for level in range(level_count):
        speed_e = es[level]
        speed_w = to_west(speed_e, mask_at + 1 + level)
        speed_n = ns[level]
        speed_s = to_south(speed_n, mask_at + 1 + level)
        for t in range(tracer_count):
            p = t * level_count + level
            x = tr[t, level]
            flux_e = speed_e * jnp.where(speed_e > 0, x, to_east(x, p)) * open_east
            flux_w = speed_w * jnp.where(speed_w > 0, to_west(x, p), x) * open_west
            flux_n = speed_n * jnp.where(speed_n > 0, x, to_north(x, p)) * open_north
            flux_s = speed_s * jnp.where(speed_s > 0, to_south(x, p), x) * open_south
            value = x - (flux_e - flux_w + flux_n - flux_s)
            if level == 0:
                surface = sums[t * row_count : (t + 1) * row_count, :] - x * last_sum
                value = value + flux_step * surface
            else:
                value = value + mix[level - 1] * done[t][-1]
            done[t].append(value * pivots[level])
    for t in range(tracer_count):
        x = done[t][-1]
        out[t, level_count - 1] = x * mask
        for level in range(level_count - 2, -1, -1):
            x = done[t][level] + ratios[level] * x
            out[t, level] = x * mask


def body(
    tracers,
    east_speed,
    north_speed,
    mixing_coef,
    ocean_mask,
    fold_map,
    atmos_state,
    atmos_coef,
    xgrid_cell,
    xgrid_atm,
    xgrid_owner,
    xgrid_weight,
):
    tracer_count, level_count, row_count, cols = tracers.shape
    lon_count = lax.axis_size("lon")
    lat_count = lax.axis_size("lat")
    plane_count = tracer_count * level_count
    blocks = atmos_coef.shape[0] // LANES
    base = (tracer_count + 1) * blocks
    pad = -(-(plane_count + 1) // 8) * 8
    north_pad = -(-(plane_count + 1 + level_count) // 8) * 8
    f32 = jnp.float32
    vmem = pl.BlockSpec(memory_space=pltpu.VMEM)
    gat, north, south, east, west = pl.pallas_call(
        pack_kernel,
        out_shape=(
            jax.ShapeDtypeStruct((base + pad, cols), f32),
            jax.ShapeDtypeStruct((north_pad, cols), f32),
            jax.ShapeDtypeStruct((pad, cols), f32),
            jax.ShapeDtypeStruct((row_count, cols), f32),
            jax.ShapeDtypeStruct((row_count, cols), f32),
        ),
        in_specs=[vmem] * 6,
        out_specs=(vmem,) * 5,
        name="pack_edges",
    )(tracers, east_speed, north_speed, ocean_mask, atmos_state, atmos_coef.reshape(blocks, LANES))
    gathered = lax.all_gather(gat, "lon", axis=0, tiled=False)
    up_lat = [(i, i + 1) for i in range(lat_count - 1)]
    down_lat = [(j, i) for i, j in up_lat]
    up_lon = [(i, (i + 1) % lon_count) for i in range(lon_count)]
    down_lon = [(j, i) for i, j in up_lon]
    from_south = lax.ppermute(north, "lat", up_lat)
    from_north = lax.ppermute(south, "lat", down_lat)
    from_west = lax.ppermute(east, "lon", up_lon)
    from_east = lax.ppermute(west, "lon", down_lon)
    rows = xgrid_cell.shape[0] // LANES
    return pl.pallas_call(
        main_kernel,
        out_shape=jax.ShapeDtypeStruct(tracers.shape, f32),
        in_specs=[vmem] * 15,
        out_specs=vmem,
        scratch_shapes=[
            pltpu.VMEM(((tracer_count + 1) * LANES, 2 * lon_count * blocks), jnp.bfloat16),
            pltpu.VMEM((2 * (tracer_count + 1) * row_count, cols), f32),
            pltpu.VMEM((pad, cols), f32),
        ],
        name="exchange_and_solve",
    )(
        tracers, east_speed, north_speed, mixing_coef, ocean_mask, fold_map.reshape(1, cols),
        gathered, from_south, from_north, from_west, from_east,
        xgrid_cell.reshape(rows, LANES), xgrid_atm.reshape(rows, LANES),
        xgrid_owner.reshape(rows, LANES), xgrid_weight.reshape(rows, LANES),
    )


def solution(mesh):
    in_specs = (
        P(None, None, "lat", "lon"),
        P(None, "lat", "lon"),
        P(None, "lat", "lon"),
        P(None, "lat", "lon"),
        P("lat", "lon"),
        P("lon"),
        P(None, ("lon", "lat")),
        P(("lon", "lat")),
        P(("lon", "lat")),
        P(("lon", "lat")),
        P(("lon", "lat"), None),
        P(("lon", "lat")),
    )
    out_specs = P(None, None, "lat", "lon")
    return jax.shard_map(body, mesh=mesh, in_specs=in_specs, out_specs=out_specs, check_vma=False)
```

```python
import jax
import jax.numpy as jnp
from jax import lax
from jax.experimental import pallas as pl
from jax.experimental.pallas import tpu as pltpu
from jax.sharding import PartitionSpec as P

flux_step = 0.5
LANES = 128
WIDE = 512
Y_GROUPS = 4


def pack_kernel(tr, es, ns, om, state, coef, air, north, south, east, west):
    tracer_count, level_count, row_count, cols = tr.shape
    blocks = state.shape[1] // LANES
    for t in range(tracer_count):
        for h in range(blocks):
            air[t * blocks + h : t * blocks + h + 1, :] = state[t : t + 1, h * LANES : (h + 1) * LANES]
    air[tracer_count * blocks : (tracer_count + 1) * blocks, :] = coef[...]
    plane_count = tracer_count * level_count
    lane = lax.broadcasted_iota(jnp.int32, (row_count, cols), 1)
    mask = om[...].astype(jnp.float32)
    north[...] = jnp.zeros_like(north)
    south[...] = jnp.zeros_like(south)
    first = jnp.zeros((row_count, cols), jnp.float32)
    last = jnp.zeros((row_count, cols), jnp.float32)
    for p in range(plane_count + 1 + level_count):
        if p < plane_count:
            plane = tr[p // level_count, p % level_count]
            north_plane = plane
        elif p == plane_count:
            plane = mask
            north_plane = plane
        else:
            plane = es[p - plane_count - 1]
            north_plane = ns[p - plane_count - 1]
        north[p : p + 1, :] = north_plane[row_count - 1 : row_count, :]
        last = jnp.where(lane == p, plane[:, cols - 1 : cols], last)
        if p <= plane_count:
            south[p : p + 1, :] = plane[0:1, :]
            first = jnp.where(lane == p, plane[:, 0:1], first)
    east[...] = last
    west[...] = first


def exchange_kernel(
    air, north, south, east, west,
    air_all, top_all, from_south, from_north, from_west, from_east,
    send_air, recv_air, send_top, recv_top, send_edge, recv_edge, own,
):
    z_count = air_all.shape[0]
    lon_count = z_count * Y_GROUPS
    lat_count = lax.axis_size("lat")
    lon = lax.axis_index("lon")
    lat = lax.axis_index("lat")
    z = lax.rem(lon, z_count)
    y_base = lon - z
    z_right = {"lon": y_base + lax.rem(z + 1, z_count)}
    z_left = {"lon": y_base + lax.rem(z + z_count - 1, z_count)}
    y_to = [{"lon": lax.rem(lon + d * z_count, lon_count)} for d in range(Y_GROUPS)]
    lon_right = {"lon": lax.rem(lon + 1, lon_count)}
    lon_left = {"lon": lax.rem(lon + lon_count - 1, lon_count)}
    lat_up = {"lat": lax.rem(lat + 1, lat_count)}
    lat_down = {"lat": lax.rem(lat + lat_count - 1, lat_count)}
    partners = [z_right, z_left, lon_right, lon_left, lat_up, lat_down] + y_to[1:]
    is_top = lat == lat_count - 1
    mesh_ids = pl.DeviceIdType.MESH

    barrier = pltpu.get_barrier_semaphore()
    for partner in partners:
        pl.semaphore_signal(barrier, inc=1, device_id=partner, device_id_type=mesh_ids)
    pl.semaphore_wait(barrier, len(partners))

    edges = []
    for i, (src, dst, target) in enumerate(
        ((north, from_south, lat_up), (south, from_north, lat_down),
         (east, from_west, lon_right), (west, from_east, lon_left))
    ):
        edges.append(
            pltpu.make_async_remote_copy(
                src_ref=src, dst_ref=dst, send_sem=send_edge.at[i], recv_sem=recv_edge.at[i],
                device_id=target, device_id_type=mesh_ids,
            )
        )

    right_steps = z_count // 2
    left_steps = z_count - 1 - right_steps
    pad = top_all.shape[2]

    def flow(first, slots, send, recv):
        def copy(slot, d):
            if slot == 0:
                src, target = first, y_to[d]
            elif slot <= right_steps:
                before = slot - 1
                src = first if before == 0 and d == 0 else slots.at[before, d]
                target = z_right
            else:
                before = (slot + 1) % z_count
                src = first if before == 0 and d == 0 else slots.at[before, d]
                target = z_left
            return pltpu.make_async_remote_copy(
                src_ref=src, dst_ref=slots.at[slot, d], send_sem=send.at[slot, d],
                recv_sem=recv.at[slot, d], device_id=target, device_id_type=mesh_ids,
            )

        return copy

    air_flow = flow(air, air_all, send_air, recv_air)
    top_flow = flow(north.at[0:pad], top_all, send_top, recv_top)
    air_own = pltpu.make_async_copy(air, air_all.at[0, 0], own.at[0])
    top_own = pltpu.make_async_copy(north.at[0:pad], top_all.at[0, 0], own.at[1])

    def begin(copy):
        for d in range(1, Y_GROUPS):
            copy(0, d).start()
        copy(1, 0).start()
        copy(z_count - 1, 0).start()

    def advance(copy, step):
        for d in range(Y_GROUPS):
            if step == 0:
                if d > 0:
                    copy(0, d).wait_recv()
                    copy(1, d).start()
                    copy(z_count - 1, d).start()
                continue
            copy(step, d).wait_recv()
            if step < right_steps:
                copy(step + 1, d).start()
            if step <= left_steps:
                copy(z_count - step, d).wait_recv()
                if step < left_steps:
                    copy(z_count - step - 1, d).start()

    def finish(copy):
        for slot in range(z_count):
            for d in range(Y_GROUPS):
                if slot or d:
                    copy(slot, d).wait_send()

    for edge in edges:
        edge.start()
    begin(air_flow)
    air_own.start()

    @pl.when(is_top)
    def _():
        begin(top_flow)
        top_own.start()

    for step in range(right_steps + 1):
        advance(air_flow, step)

        @pl.when(is_top)
        def _():
            advance(top_flow, step)

    finish(air_flow)
    air_own.wait()

    @pl.when(is_top)
    def _():
        finish(top_flow)
        top_own.wait()

    for edge in edges:
        edge.wait()


def split(x, pieces):
    out = []
    for i in range(pieces):
        top = x.astype(jnp.bfloat16)
        out.append(top)
        x = x - top.astype(jnp.float32)
    return out


def main_kernel(
    tr, es, ns, mix, om, fold, gat, top_rows, from_south, from_north, from_west, from_east,
    cell, atm, owner, weight, out, table, total, mirror,
):
    tracer_count, level_count, row_count, cols = tr.shape
    lon_count = gat.shape[0]
    values = tracer_count + 1
    blocks = 1024 // LANES
    base = values * blocks
    hi_count = lon_count * blocks
    z_count = lon_count // Y_GROUPS
    lon = lax.axis_index("lon")
    my_z = lax.rem(lon, z_count)
    my_y = lax.div(lon, z_count)
    plane_count = tracer_count * level_count
    lat_count = lax.axis_size("lat")
    is_top = lax.axis_index("lat") == lat_count - 1
    is_bottom = lax.axis_index("lat") == 0

    def place_of(owners):
        y = jnp.zeros_like(owners)
        for group in range(1, Y_GROUPS):
            y = y + (owners >= group * z_count).astype(jnp.int32)
        far_z = my_z - (owners - y * z_count)
        far_y = my_y - y
        far_z = jnp.where(far_z < 0, far_z + z_count, far_z)
        far_y = jnp.where(far_y < 0, far_y + Y_GROUPS, far_y)
        return far_z * Y_GROUPS + far_y

    coef = gat[:, tracer_count * blocks : base, :].reshape(hi_count, LANES)
    for t in range(values):
        if t < tracer_count:
            block = gat[:, t * blocks : (t + 1) * blocks, :].reshape(hi_count, LANES) * coef
        else:
            block = coef
        turned = block.T
        for i, piece in enumerate(split(turned, 2)):
            table[t * LANES : (t + 1) * LANES, i * hi_count : (i + 1) * hi_count] = piece

    total[...] = jnp.zeros_like(total)
    rows_each = WIDE // LANES

    def step(k, carry):
        def rows(ref):
            return jnp.concatenate(
                [ref[pl.ds(k * rows_each + i, 1), :] for i in range(rows_each)], axis=1
            )

        cells, atms, owners, weights = rows(cell), rows(atm), rows(owner), rows(weight)
        hi = place_of(owners) * blocks + (atms >> 7)
        lo = atms & (LANES - 1)
        hi_hot = (lax.broadcasted_iota(jnp.int32, (hi_count, WIDE), 0) == hi).astype(
            jnp.float32
        ).astype(jnp.bfloat16)
        picked = jnp.dot(
            table[...], jnp.concatenate([hi_hot, hi_hot], axis=0),
            preferred_element_type=jnp.float32,
        )
        lane_row = lax.broadcasted_iota(jnp.int32, (LANES, WIDE), 0)
        lo_mask = lane_row == lo
        col_hot = (lane_row == (cells & (cols - 1))).astype(jnp.float32).astype(jnp.bfloat16)
        row_mask = lax.broadcasted_iota(jnp.int32, (row_count, WIDE), 0) == (cells >> 7)
        parts = []
        for t in range(values):
            chosen = jnp.where(lo_mask, picked[t * LANES : (t + 1) * LANES, :], 0.0)
            value = jnp.sum(chosen, axis=0, keepdims=True) * weights
            parts.append(jnp.where(row_mask, value, 0.0))
        left = jnp.concatenate(parts, axis=0)
        left = jnp.concatenate(split(left, 2), axis=0)
        total[...] += lax.dot_general(
            left, col_hot, (((1,), (1,)), ((), ())), preferred_element_type=jnp.float32
        )
        return carry

    lax.fori_loop(0, cell.shape[0] // rows_each, step, 0)

    mirror[...] = from_north[...]

    @pl.when(is_top)
    def _():
        lane_row = lax.broadcasted_iota(jnp.int32, (2 * LANES, LANES), 0)
        pad = mirror.shape[0]
        spot = place_of(fold[...] >> 7) * LANES + (fold[...] & (LANES - 1))

        def fold_step(k, acc):
            both = jnp.concatenate(
                [top_rows[2 * k], top_rows[2 * k + 1]], axis=1
            )
            hot = (lane_row == spot - k * (2 * LANES)).astype(jnp.float32).astype(jnp.bfloat16)
            return acc + jnp.dot(
                jnp.concatenate(split(both, 3), axis=0), hot, preferred_element_type=jnp.float32
            )

        acc = lax.fori_loop(
            0, lon_count // 2, fold_step, jnp.zeros((3 * pad, LANES), jnp.float32)
        )
        mirror[...] = acc[:pad] + acc[pad : 2 * pad] + acc[2 * pad :]

    mask = om[...].astype(jnp.float32)
    lane = lax.broadcasted_iota(jnp.int32, (row_count, cols), 1)
    row = lax.broadcasted_iota(jnp.int32, (row_count, cols), 0)
    west_cols = from_west[...]
    east_cols = from_east[...]
    south_rows = jnp.where(is_bottom, 0.0, from_south[...])

    def to_west(x, p):
        return jnp.where(lane == 0, west_cols[:, p : p + 1], pltpu.roll(x, 1, 1))

    def to_east(x, p):
        return jnp.where(lane == cols - 1, east_cols[:, p : p + 1], pltpu.roll(x, cols - 1, 1))

    def to_south(x, p):
        return jnp.where(row == 0, south_rows[p : p + 1, :], pltpu.roll(x, 1, 0))

    def to_north(x, p):
        return jnp.where(row == row_count - 1, mirror[p : p + 1, :], pltpu.roll(x, row_count - 1, 0))

    mask_at = plane_count
    open_east = mask * to_east(mask, mask_at)
    open_west = to_west(mask, mask_at) * mask
    open_north = mask * to_north(mask, mask_at)
    open_south = to_south(mask, mask_at) * mask
    pivots = []
    ratios = []
    for level in range(level_count):
        lower = mix[level] if level < level_count - 1 else jnp.zeros_like(mask)
        if level == 0:
            pivot = 1.0 + lower
        else:
            pivot = 1.0 + mix[level - 1] + lower - mix[level - 1] * ratios[-1]
        inverse = 1.0 / pivot
        pivots.append(inverse)
        ratios.append(lower * inverse)
    done = [[] for _ in range(tracer_count)]
    lines = tracer_count + 1
    half = lines * row_count
    sums = total[0:half, :] + total[half : 2 * half, :]
    last_sum = sums[tracer_count * row_count :, :]
    for level in range(level_count):
        speed_e = es[level]
        speed_w = to_west(speed_e, mask_at + 1 + level)
        speed_n = ns[level]
        speed_s = to_south(speed_n, mask_at + 1 + level)
        for t in range(tracer_count):
            p = t * level_count + level
            x = tr[t, level]
            flux_e = speed_e * jnp.where(speed_e > 0, x, to_east(x, p)) * open_east
            flux_w = speed_w * jnp.where(speed_w > 0, to_west(x, p), x) * open_west
            flux_n = speed_n * jnp.where(speed_n > 0, x, to_north(x, p)) * open_north
            flux_s = speed_s * jnp.where(speed_s > 0, to_south(x, p), x) * open_south
            value = x - (flux_e - flux_w + flux_n - flux_s)
            if level == 0:
                surface = sums[t * row_count : (t + 1) * row_count, :] - x * last_sum
                value = value + flux_step * surface
            else:
                value = value + mix[level - 1] * done[t][-1]
            done[t].append(value * pivots[level])
    for t in range(tracer_count):
        x = done[t][-1]
        out[t, level_count - 1] = x * mask
        for level in range(level_count - 2, -1, -1):
            x = done[t][level] + ratios[level] * x
            out[t, level] = x * mask


def body(
    tracers,
    east_speed,
    north_speed,
    mixing_coef,
    ocean_mask,
    fold_map,
    atmos_state,
    atmos_coef,
    xgrid_cell,
    xgrid_atm,
    xgrid_owner,
    xgrid_weight,
):
    tracer_count, level_count, row_count, cols = tracers.shape
    lon_count = lax.axis_size("lon")
    lat_count = lax.axis_size("lat")
    plane_count = tracer_count * level_count
    blocks = atmos_coef.shape[0] // LANES
    base = (tracer_count + 1) * blocks
    pad = -(-(plane_count + 1) // 8) * 8
    north_pad = -(-(plane_count + 1 + level_count) // 8) * 8
    f32 = jnp.float32
    vmem = pl.BlockSpec(memory_space=pltpu.VMEM)
    edges = (
        jax.ShapeDtypeStruct((north_pad, cols), f32),
        jax.ShapeDtypeStruct((pad, cols), f32),
        jax.ShapeDtypeStruct((row_count, cols), f32),
        jax.ShapeDtypeStruct((row_count, cols), f32),
    )
    air, north, south, east, west = pl.pallas_call(
        pack_kernel,
        out_shape=(jax.ShapeDtypeStruct((base, cols), f32),) + edges,
        in_specs=[vmem] * 6,
        out_specs=(vmem,) * 5,
        name="pack_edges",
    )(tracers, east_speed, north_speed, ocean_mask, atmos_state, atmos_coef.reshape(blocks, LANES))
    z_count = lon_count // Y_GROUPS
    spots = (z_count, Y_GROUPS)
    air_all, top_all, from_south, from_north, from_west, from_east = pl.pallas_call(
        exchange_kernel,
        out_shape=(
            jax.ShapeDtypeStruct(spots + (base, cols), f32),
            jax.ShapeDtypeStruct(spots + (pad, cols), f32),
        ) + edges,
        in_specs=[vmem] * 5,
        out_specs=(vmem,) * 6,
        scratch_shapes=[
            pltpu.SemaphoreType.DMA(spots),
            pltpu.SemaphoreType.DMA(spots),
            pltpu.SemaphoreType.DMA(spots),
            pltpu.SemaphoreType.DMA(spots),
            pltpu.SemaphoreType.DMA((4,)),
            pltpu.SemaphoreType.DMA((4,)),
            pltpu.SemaphoreType.DMA((2,)),
        ],
        compiler_params=pltpu.CompilerParams(collective_id=0, has_side_effects=True),
        name="exchange_edges",
    )(air, north, south, east, west)
    rows = xgrid_cell.shape[0] // LANES
    return pl.pallas_call(
        main_kernel,
        out_shape=jax.ShapeDtypeStruct(tracers.shape, f32),
        in_specs=[vmem] * 16,
        out_specs=vmem,
        scratch_shapes=[
            pltpu.VMEM(((tracer_count + 1) * LANES, 2 * lon_count * blocks), jnp.bfloat16),
            pltpu.VMEM((2 * (tracer_count + 1) * row_count, cols), f32),
            pltpu.VMEM((pad, cols), f32),
        ],
        name="exchange_and_solve",
    )(
        tracers, east_speed, north_speed, mixing_coef, ocean_mask, fold_map.reshape(1, cols),
        air_all.reshape(lon_count, base, cols), top_all.reshape(lon_count, pad, cols), from_south, from_north, from_west, from_east,
        xgrid_cell.reshape(rows, LANES), xgrid_atm.reshape(rows, LANES),
        xgrid_owner.reshape(rows, LANES), xgrid_weight.reshape(rows, LANES),
    )


def solution(mesh):
    in_specs = (
        P(None, None, "lat", "lon"),
        P(None, "lat", "lon"),
        P(None, "lat", "lon"),
        P(None, "lat", "lon"),
        P("lat", "lon"),
        P("lon"),
        P(None, ("lon", "lat")),
        P(("lon", "lat")),
        P(("lon", "lat")),
        P(("lon", "lat")),
        P(("lon", "lat"), None),
        P(("lon", "lat")),
    )
    out_specs = P(None, None, "lat", "lon")
    return jax.shard_map(body, mesh=mesh, in_specs=in_specs, out_specs=out_specs, check_vma=False)
```

```python
import jax
import jax.numpy as jnp
from jax import lax
from jax.experimental import pallas as pl
from jax.experimental.pallas import tpu as pltpu
from jax.sharding import PartitionSpec as P

flux_step = 0.5
LANES = 128
WIDE = 2048
FOLD_STEP = 16
Y_GROUPS = 4


def pack_kernel(tr, es, ns, om, state, coef, air, north, south, east, west):
    tracer_count, level_count, row_count, cols = tr.shape
    blocks = state.shape[1] // LANES
    for t in range(tracer_count):
        for h in range(blocks):
            air[t * blocks + h : t * blocks + h + 1, :] = state[t : t + 1, h * LANES : (h + 1) * LANES]
    air[tracer_count * blocks : (tracer_count + 1) * blocks, :] = coef[...]
    plane_count = tracer_count * level_count
    lane = lax.broadcasted_iota(jnp.int32, (row_count, cols), 1)
    mask = om[...].astype(jnp.float32)
    north[...] = jnp.zeros_like(north)
    south[...] = jnp.zeros_like(south)
    first = jnp.zeros((row_count, cols), jnp.float32)
    last = jnp.zeros((row_count, cols), jnp.float32)
    for p in range(plane_count + 1 + level_count):
        if p < plane_count:
            plane = tr[p // level_count, p % level_count]
            north_plane = plane
        elif p == plane_count:
            plane = mask
            north_plane = plane
        else:
            plane = es[p - plane_count - 1]
            north_plane = ns[p - plane_count - 1]
        north[p : p + 1, :] = north_plane[row_count - 1 : row_count, :]
        last = jnp.where(lane == p, plane[:, cols - 1 : cols], last)
        if p <= plane_count:
            south[p : p + 1, :] = plane[0:1, :]
            first = jnp.where(lane == p, plane[:, 0:1], first)
    east[...] = last
    west[...] = first


def exchange_kernel(
    air, north, south, east, west,
    air_all, top_all, from_south, from_north, from_west, from_east,
    send_air, recv_air, send_top, recv_top, send_edge, recv_edge, own,
):
    z_count = air_all.shape[0]
    lon_count = z_count * Y_GROUPS
    lat_count = lax.axis_size("lat")
    lon = lax.axis_index("lon")
    lat = lax.axis_index("lat")
    z = lax.rem(lon, z_count)
    y_base = lon - z
    z_right = {"lon": y_base + lax.rem(z + 1, z_count)}
    z_left = {"lon": y_base + lax.rem(z + z_count - 1, z_count)}
    y_to = [{"lon": lax.rem(lon + d * z_count, lon_count)} for d in range(Y_GROUPS)]
    lon_right = {"lon": lax.rem(lon + 1, lon_count)}
    lon_left = {"lon": lax.rem(lon + lon_count - 1, lon_count)}
    lat_up = {"lat": lax.rem(lat + 1, lat_count)}
    lat_down = {"lat": lax.rem(lat + lat_count - 1, lat_count)}
    partners = [z_right, z_left, lon_right, lon_left, lat_up, lat_down] + y_to[1:]
    is_top = lat == lat_count - 1
    mesh_ids = pl.DeviceIdType.MESH

    barrier = pltpu.get_barrier_semaphore()
    for partner in partners:
        pl.semaphore_signal(barrier, inc=1, device_id=partner, device_id_type=mesh_ids)
    pl.semaphore_wait(barrier, len(partners))

    edges = []
    for i, (src, dst, target) in enumerate(
        ((north, from_south, lat_up), (south, from_north, lat_down),
         (east, from_west, lon_right), (west, from_east, lon_left))
    ):
        edges.append(
            pltpu.make_async_remote_copy(
                src_ref=src, dst_ref=dst, send_sem=send_edge.at[i], recv_sem=recv_edge.at[i],
                device_id=target, device_id_type=mesh_ids,
            )
        )

    right_steps = z_count // 2
    left_steps = z_count - 1 - right_steps
    pad = top_all.shape[2]

    def flow(first, slots, send, recv):
        def copy(slot, d):
            if slot == 0:
                src, target = first, y_to[d]
            elif slot <= right_steps:
                before = slot - 1
                src = first if before == 0 and d == 0 else slots.at[before, d]
                target = z_right
            else:
                before = (slot + 1) % z_count
                src = first if before == 0 and d == 0 else slots.at[before, d]
                target = z_left
            return pltpu.make_async_remote_copy(
                src_ref=src, dst_ref=slots.at[slot, d], send_sem=send.at[slot, d],
                recv_sem=recv.at[slot, d], device_id=target, device_id_type=mesh_ids,
            )

        return copy

    air_flow = flow(air, air_all, send_air, recv_air)
    top_flow = flow(north.at[0:pad], top_all, send_top, recv_top)
    air_own = pltpu.make_async_copy(air, air_all.at[0, 0], own.at[0])
    top_own = pltpu.make_async_copy(north.at[0:pad], top_all.at[0, 0], own.at[1])

    def begin(copy):
        for d in range(1, Y_GROUPS):
            copy(0, d).start()
        copy(1, 0).start()
        copy(z_count - 1, 0).start()

    def advance(copy, step, d):
        if step == 0:
            if d > 0:
                copy(0, d).wait_recv()
                copy(1, d).start()
                copy(z_count - 1, d).start()
            return
        copy(step, d).wait_recv()
        if step < right_steps:
            copy(step + 1, d).start()
        if step <= left_steps:
            copy(z_count - step, d).wait_recv()
            if step < left_steps:
                copy(z_count - step - 1, d).start()

    order = []
    for d in range(Y_GROUPS):
        delay = 0.5 + 0.7 * min(d, Y_GROUPS - d) if d else 0.0
        for step in range(right_steps + 1):
            order.append((step + delay, d, step, False))
            order.append((step + delay + 0.6, d, step, True))
    order.sort()

    def finish(copy):
        for slot in range(z_count):
            for d in range(Y_GROUPS):
                if slot or d:
                    copy(slot, d).wait_send()

    for edge in edges:
        edge.start()
    begin(air_flow)
    air_own.start()

    @pl.when(is_top)
    def _():
        begin(top_flow)
        top_own.start()

    for _, d, step, is_fold in order:
        if is_fold:

            @pl.when(is_top)
            def _():
                advance(top_flow, step, d)

        else:
            advance(air_flow, step, d)

    finish(air_flow)
    air_own.wait()

    @pl.when(is_top)
    def _():
        finish(top_flow)
        top_own.wait()

    for edge in edges:
        edge.wait()


def split(x, pieces):
    out = []
    for i in range(pieces):
        top = x.astype(jnp.bfloat16)
        out.append(top)
        x = x - top.astype(jnp.float32)
    return out


def main_kernel(
    tr, es, ns, mix, om, fold, gat, top_rows, from_south, from_north, from_west, from_east,
    cell, atm, owner, weight, out, table, total, mirror,
):
    tracer_count, level_count, row_count, cols = tr.shape
    lon_count = gat.shape[0]
    values = tracer_count + 1
    blocks = 1024 // LANES
    base = values * blocks
    hi_count = lon_count * blocks
    z_count = lon_count // Y_GROUPS
    lon = lax.axis_index("lon")
    my_z = lax.rem(lon, z_count)
    my_y = lax.div(lon, z_count)
    plane_count = tracer_count * level_count
    lat_count = lax.axis_size("lat")
    is_top = lax.axis_index("lat") == lat_count - 1
    is_bottom = lax.axis_index("lat") == 0

    def place_of(owners):
        y = jnp.zeros_like(owners)
        for group in range(1, Y_GROUPS):
            y = y + (owners >= group * z_count).astype(jnp.int32)
        far_z = my_z - (owners - y * z_count)
        far_y = my_y - y
        far_z = jnp.where(far_z < 0, far_z + z_count, far_z)
        far_y = jnp.where(far_y < 0, far_y + Y_GROUPS, far_y)
        return far_z * Y_GROUPS + far_y

    coef = gat[:, tracer_count * blocks : base, :].reshape(hi_count, LANES)
    for t in range(values):
        if t < tracer_count:
            block = gat[:, t * blocks : (t + 1) * blocks, :].reshape(hi_count, LANES) * coef
        else:
            block = coef
        turned = block.T
        for i, piece in enumerate(split(turned, 2)):
            table[t * LANES : (t + 1) * LANES, i * hi_count : (i + 1) * hi_count] = piece

    total[...] = jnp.zeros_like(total)
    rows_each = WIDE // LANES

    def step(k, carry):
        def rows(ref):
            return jnp.concatenate(
                [ref[pl.ds(k * rows_each + i, 1), :] for i in range(rows_each)], axis=1
            )

        cells, atms, owners, weights = rows(cell), rows(atm), rows(owner), rows(weight)
        hi = place_of(owners) * blocks + (atms >> 7)
        lo = atms & (LANES - 1)
        hi_hot = (lax.broadcasted_iota(jnp.int32, (hi_count, WIDE), 0) == hi).astype(
            jnp.float32
        ).astype(jnp.bfloat16)
        picked = jnp.dot(
            table[...], jnp.concatenate([hi_hot, hi_hot], axis=0),
            preferred_element_type=jnp.float32,
        )
        lane_row = lax.broadcasted_iota(jnp.int32, (LANES, WIDE), 0)
        lo_mask = lane_row == lo
        col_hot = (lane_row == (cells & (cols - 1))).astype(jnp.float32).astype(jnp.bfloat16)
        row_mask = lax.broadcasted_iota(jnp.int32, (row_count, WIDE), 0) == (cells >> 7)
        parts = []
        for t in range(values):
            chosen = jnp.where(lo_mask, picked[t * LANES : (t + 1) * LANES, :], 0.0)
            value = jnp.sum(chosen, axis=0, keepdims=True) * weights
            parts.append(jnp.where(row_mask, value, 0.0))
        left = jnp.concatenate(parts, axis=0)
        left = jnp.concatenate(split(left, 2), axis=0)
        total[...] += lax.dot_general(
            left, col_hot, (((1,), (1,)), ((), ())), preferred_element_type=jnp.float32
        )
        return carry

    lax.fori_loop(0, cell.shape[0] // rows_each, step, 0)

    mirror[...] = from_north[...]

    @pl.when(is_top)
    def _():
        depth = FOLD_STEP * LANES
        lane_row = lax.broadcasted_iota(jnp.int32, (depth, LANES), 0)
        pad = mirror.shape[0]
        spot = place_of(fold[...] >> 7) * LANES + (fold[...] & (LANES - 1))

        def fold_step(k, acc):
            block = jnp.concatenate(
                [top_rows[FOLD_STEP * k + i] for i in range(FOLD_STEP)], axis=1
            )
            hot = (lane_row == spot - k * depth).astype(jnp.float32).astype(jnp.bfloat16)
            return acc + jnp.dot(
                jnp.concatenate(split(block, 2), axis=0), hot, preferred_element_type=jnp.float32
            )

        acc = lax.fori_loop(
            0, lon_count // FOLD_STEP, fold_step, jnp.zeros((2 * pad, LANES), jnp.float32)
        )
        mirror[...] = acc[:pad] + acc[pad:]

    mask = om[...].astype(jnp.float32)
    lane = lax.broadcasted_iota(jnp.int32, (row_count, cols), 1)
    row = lax.broadcasted_iota(jnp.int32, (row_count, cols), 0)
    west_cols = from_west[...]
    east_cols = from_east[...]
    south_rows = jnp.where(is_bottom, 0.0, from_south[...])

    def to_west(x, p):
        return jnp.where(lane == 0, west_cols[:, p : p + 1], pltpu.roll(x, 1, 1))

    def to_east(x, p):
        return jnp.where(lane == cols - 1, east_cols[:, p : p + 1], pltpu.roll(x, cols - 1, 1))

    def to_south(x, p):
        return jnp.where(row == 0, south_rows[p : p + 1, :], pltpu.roll(x, 1, 0))

    def to_north(x, p):
        return jnp.where(row == row_count - 1, mirror[p : p + 1, :], pltpu.roll(x, row_count - 1, 0))

    mask_at = plane_count
    open_east = mask * to_east(mask, mask_at)
    open_west = to_west(mask, mask_at) * mask
    open_north = mask * to_north(mask, mask_at)
    open_south = to_south(mask, mask_at) * mask
    pivots = []
    ratios = []
    for level in range(level_count):
        lower = mix[level] if level < level_count - 1 else jnp.zeros_like(mask)
        if level == 0:
            pivot = 1.0 + lower
        else:
            pivot = 1.0 + mix[level - 1] + lower - mix[level - 1] * ratios[-1]
        inverse = 1.0 / pivot
        pivots.append(inverse)
        ratios.append(lower * inverse)
    done = [[] for _ in range(tracer_count)]
    lines = tracer_count + 1
    half = lines * row_count
    sums = total[0:half, :] + total[half : 2 * half, :]
    last_sum = sums[tracer_count * row_count :, :]
    for level in range(level_count):
        speed_e = es[level]
        speed_w = to_west(speed_e, mask_at + 1 + level)
        speed_n = ns[level]
        speed_s = to_south(speed_n, mask_at + 1 + level)
        for t in range(tracer_count):
            p = t * level_count + level
            x = tr[t, level]
            flux_e = speed_e * jnp.where(speed_e > 0, x, to_east(x, p)) * open_east
            flux_w = speed_w * jnp.where(speed_w > 0, to_west(x, p), x) * open_west
            flux_n = speed_n * jnp.where(speed_n > 0, x, to_north(x, p)) * open_north
            flux_s = speed_s * jnp.where(speed_s > 0, to_south(x, p), x) * open_south
            value = x - (flux_e - flux_w + flux_n - flux_s)
            if level == 0:
                surface = sums[t * row_count : (t + 1) * row_count, :] - x * last_sum
                value = value + flux_step * surface
            else:
                value = value + mix[level - 1] * done[t][-1]
            done[t].append(value * pivots[level])
    for t in range(tracer_count):
        x = done[t][-1]
        out[t, level_count - 1] = x * mask
        for level in range(level_count - 2, -1, -1):
            x = done[t][level] + ratios[level] * x
            out[t, level] = x * mask


def body(
    tracers,
    east_speed,
    north_speed,
    mixing_coef,
    ocean_mask,
    fold_map,
    atmos_state,
    atmos_coef,
    xgrid_cell,
    xgrid_atm,
    xgrid_owner,
    xgrid_weight,
):
    tracer_count, level_count, row_count, cols = tracers.shape
    lon_count = lax.axis_size("lon")
    lat_count = lax.axis_size("lat")
    plane_count = tracer_count * level_count
    blocks = atmos_coef.shape[0] // LANES
    base = (tracer_count + 1) * blocks
    pad = -(-(plane_count + 1) // 8) * 8
    north_pad = -(-(plane_count + 1 + level_count) // 8) * 8
    f32 = jnp.float32
    vmem = pl.BlockSpec(memory_space=pltpu.VMEM)
    edges = (
        jax.ShapeDtypeStruct((north_pad, cols), f32),
        jax.ShapeDtypeStruct((pad, cols), f32),
        jax.ShapeDtypeStruct((row_count, cols), f32),
        jax.ShapeDtypeStruct((row_count, cols), f32),
    )
    air, north, south, east, west = pl.pallas_call(
        pack_kernel,
        out_shape=(jax.ShapeDtypeStruct((base, cols), f32),) + edges,
        in_specs=[vmem] * 6,
        out_specs=(vmem,) * 5,
        name="pack_edges",
    )(tracers, east_speed, north_speed, ocean_mask, atmos_state, atmos_coef.reshape(blocks, LANES))
    z_count = lon_count // Y_GROUPS
    spots = (z_count, Y_GROUPS)
    air_all, top_all, from_south, from_north, from_west, from_east = pl.pallas_call(
        exchange_kernel,
        out_shape=(
            jax.ShapeDtypeStruct(spots + (base, cols), f32),
            jax.ShapeDtypeStruct(spots + (pad, cols), f32),
        ) + edges,
        in_specs=[vmem] * 5,
        out_specs=(vmem,) * 6,
        scratch_shapes=[
            pltpu.SemaphoreType.DMA(spots),
            pltpu.SemaphoreType.DMA(spots),
            pltpu.SemaphoreType.DMA(spots),
            pltpu.SemaphoreType.DMA(spots),
            pltpu.SemaphoreType.DMA((4,)),
            pltpu.SemaphoreType.DMA((4,)),
            pltpu.SemaphoreType.DMA((2,)),
        ],
        compiler_params=pltpu.CompilerParams(collective_id=0, has_side_effects=True),
        name="exchange_edges",
    )(air, north, south, east, west)
    rows = xgrid_cell.shape[0] // LANES
    return pl.pallas_call(
        main_kernel,
        out_shape=jax.ShapeDtypeStruct(tracers.shape, f32),
        in_specs=[vmem] * 16,
        out_specs=vmem,
        scratch_shapes=[
            pltpu.VMEM(((tracer_count + 1) * LANES, 2 * lon_count * blocks), jnp.bfloat16),
            pltpu.VMEM((2 * (tracer_count + 1) * row_count, cols), f32),
            pltpu.VMEM((pad, cols), f32),
        ],
        name="exchange_and_solve",
    )(
        tracers, east_speed, north_speed, mixing_coef, ocean_mask, fold_map.reshape(1, cols),
        air_all.reshape(lon_count, base, cols), top_all.reshape(lon_count, pad, cols), from_south, from_north, from_west, from_east,
        xgrid_cell.reshape(rows, LANES), xgrid_atm.reshape(rows, LANES),
        xgrid_owner.reshape(rows, LANES), xgrid_weight.reshape(rows, LANES),
    )


def solution(mesh):
    in_specs = (
        P(None, None, "lat", "lon"),
        P(None, "lat", "lon"),
        P(None, "lat", "lon"),
        P(None, "lat", "lon"),
        P("lat", "lon"),
        P("lon"),
        P(None, ("lon", "lat")),
        P(("lon", "lat")),
        P(("lon", "lat")),
        P(("lon", "lat")),
        P(("lon", "lat"), None),
        P(("lon", "lat")),
    )
    out_specs = P(None, None, "lat", "lon")
    return jax.shard_map(body, mesh=mesh, in_specs=in_specs, out_specs=out_specs, check_vma=False)
```

```python
import jax
import jax.numpy as jnp
from jax import lax
from jax.experimental import pallas as pl
from jax.experimental.pallas import tpu as pltpu
from jax.sharding import PartitionSpec as P

flux_step = 0.5
LANES = 128
WIDE = 2048
FOLD_STEP = 16
Y_GROUPS = 4


def pack_kernel(tr, es, ns, om, state, coef, air, north, south, east, west):
    tracer_count, level_count, row_count, cols = tr.shape
    blocks = state.shape[1] // LANES
    for t in range(tracer_count):
        for h in range(blocks):
            air[t * blocks + h : t * blocks + h + 1, :] = state[t : t + 1, h * LANES : (h + 1) * LANES]
    air[tracer_count * blocks : (tracer_count + 1) * blocks, :] = coef[...]
    plane_count = tracer_count * level_count
    lane = lax.broadcasted_iota(jnp.int32, (row_count, cols), 1)
    mask = om[...].astype(jnp.float32)
    north[...] = jnp.zeros_like(north)
    south[...] = jnp.zeros_like(south)
    first = jnp.zeros((row_count, cols), jnp.float32)
    last = jnp.zeros((row_count, cols), jnp.float32)
    for p in range(plane_count + 1 + level_count):
        if p < plane_count:
            plane = tr[p // level_count, p % level_count]
            north_plane = plane
        elif p == plane_count:
            plane = mask
            north_plane = plane
        else:
            plane = es[p - plane_count - 1]
            north_plane = ns[p - plane_count - 1]
        north[p : p + 1, :] = north_plane[row_count - 1 : row_count, :]
        last = jnp.where(lane == p, plane[:, cols - 1 : cols], last)
        if p <= plane_count:
            south[p : p + 1, :] = plane[0:1, :]
            first = jnp.where(lane == p, plane[:, 0:1], first)
    east[...] = last
    west[...] = first


def exchange_kernel(
    air, north, south, east, west,
    air_all, top_all, from_south, from_north, from_west, from_east,
    send_air, recv_air, send_top, recv_top, send_edge, recv_edge, own,
):
    z_count = air_all.shape[0]
    lon_count = z_count * Y_GROUPS
    lat_count = lax.axis_size("lat")
    lon = lax.axis_index("lon")
    lat = lax.axis_index("lat")
    z = lax.rem(lon, z_count)
    y_base = lon - z
    z_right = {"lon": y_base + lax.rem(z + 1, z_count)}
    z_left = {"lon": y_base + lax.rem(z + z_count - 1, z_count)}
    y_to = [{"lon": lax.rem(lon + d * z_count, lon_count)} for d in range(Y_GROUPS)]
    lon_right = {"lon": lax.rem(lon + 1, lon_count)}
    lon_left = {"lon": lax.rem(lon + lon_count - 1, lon_count)}
    lat_up = {"lat": lax.rem(lat + 1, lat_count)}
    lat_down = {"lat": lax.rem(lat + lat_count - 1, lat_count)}
    partners = [z_right, z_left, lon_right, lon_left, lat_up, lat_down] + y_to[1:]
    is_top = lat == lat_count - 1
    mesh_ids = pl.DeviceIdType.MESH

    barrier = pltpu.get_barrier_semaphore()
    for partner in partners:
        pl.semaphore_signal(barrier, inc=1, device_id=partner, device_id_type=mesh_ids)
    pl.semaphore_wait(barrier, len(partners))

    edges = []
    for i, (src, dst, target) in enumerate(
        ((north, from_south, lat_up), (south, from_north, lat_down),
         (east, from_west, lon_right), (west, from_east, lon_left))
    ):
        edges.append(
            pltpu.make_async_remote_copy(
                src_ref=src, dst_ref=dst, send_sem=send_edge.at[i], recv_sem=recv_edge.at[i],
                device_id=target, device_id_type=mesh_ids,
            )
        )

    right_steps = z_count // 2
    left_steps = z_count - 1 - right_steps
    pad = top_all.shape[2]

    def flow(first, slots, send, recv):
        def copy(slot, d):
            if slot == 0:
                src, dst, target = first, slots.at[0, d], y_to[d]
            else:
                if slot <= right_steps:
                    before, target = slot - 1, z_right
                else:
                    before, target = (slot + 1) % z_count, z_left
                if d == 0:
                    src = first if before == 0 else slots.at[before, 0]
                    dst = slots.at[slot, 0]
                else:
                    src = slots.at[before, 1:Y_GROUPS]
                    dst = slots.at[slot, 1:Y_GROUPS]
            return pltpu.make_async_remote_copy(
                src_ref=src, dst_ref=dst, send_sem=send.at[slot, d],
                recv_sem=recv.at[slot, d], device_id=target, device_id_type=mesh_ids,
            )

        return copy

    air_flow = flow(air, air_all, send_air, recv_air)
    top_flow = flow(north.at[0:pad], top_all, send_top, recv_top)
    air_own = pltpu.make_async_copy(air, air_all.at[0, 0], own.at[0])
    top_own = pltpu.make_async_copy(north.at[0:pad], top_all.at[0, 0], own.at[1])

    def begin(copy):
        for d in range(1, Y_GROUPS):
            copy(0, d).start()
        copy(1, 0).start()
        copy(z_count - 1, 0).start()

    def advance(copy, step, d):
        if step == 0:
            if d:
                for group in range(1, Y_GROUPS):
                    copy(0, group).wait_recv()
                copy(1, 1).start()
                copy(z_count - 1, 1).start()
            return
        copy(step, d).wait_recv()
        if step < right_steps:
            copy(step + 1, d).start()
        if step <= left_steps:
            copy(z_count - step, d).wait_recv()
            if step < left_steps:
                copy(z_count - step - 1, d).start()

    order = []
    for d in (0, 1):
        delay = 1.5 * d
        for step in range(right_steps + 1):
            order.append((step + delay, d, step, False))
            order.append((step + delay + 0.6, d, step, True))
    order.sort()

    def finish(copy):
        for group in range(1, Y_GROUPS):
            copy(0, group).wait_send()
        for slot in range(1, z_count):
            copy(slot, 0).wait_send()
            copy(slot, 1).wait_send()

    for edge in edges:
        edge.start()
    begin(air_flow)
    air_own.start()

    @pl.when(is_top)
    def _():
        begin(top_flow)
        top_own.start()

    for _, d, step, is_fold in order:
        if is_fold:

            @pl.when(is_top)
            def _():
                advance(top_flow, step, d)

        else:
            advance(air_flow, step, d)

    finish(air_flow)
    air_own.wait()

    @pl.when(is_top)
    def _():
        finish(top_flow)
        top_own.wait()

    for edge in edges:
        edge.wait()


def split(x, pieces):
    out = []
    for i in range(pieces):
        top = x.astype(jnp.bfloat16)
        out.append(top)
        x = x - top.astype(jnp.float32)
    return out


def main_kernel(
    tr, es, ns, mix, om, fold, gat, top_all, from_south, from_north, from_west, from_east,
    cell, atm, owner, weight, out, table, total, mirror, top_rows, top_sem,
):
    tracer_count, level_count, row_count, cols = tr.shape
    lon_count = gat.shape[0]
    values = tracer_count + 1
    blocks = 1024 // LANES
    base = values * blocks
    hi_count = lon_count * blocks
    z_count = lon_count // Y_GROUPS
    lon = lax.axis_index("lon")
    my_z = lax.rem(lon, z_count)
    my_y = lax.div(lon, z_count)
    plane_count = tracer_count * level_count
    lat_count = lax.axis_size("lat")
    is_top = lax.axis_index("lat") == lat_count - 1
    is_bottom = lax.axis_index("lat") == 0

    top_copy = pltpu.make_async_copy(top_all, top_rows, top_sem)

    @pl.when(is_top)
    def _():
        top_copy.start()

    def place_of(owners):
        y = jnp.zeros_like(owners)
        for group in range(1, Y_GROUPS):
            y = y + (owners >= group * z_count).astype(jnp.int32)
        far_z = my_z - (owners - y * z_count)
        far_y = my_y - y
        far_z = jnp.where(far_z < 0, far_z + z_count, far_z)
        far_y = jnp.where(far_y < 0, far_y + Y_GROUPS, far_y)
        return far_z * Y_GROUPS + far_y

    coef = gat[:, tracer_count * blocks : base, :].reshape(hi_count, LANES)
    for t in range(values):
        if t < tracer_count:
            block = gat[:, t * blocks : (t + 1) * blocks, :].reshape(hi_count, LANES) * coef
        else:
            block = coef
        turned = block.T
        for i, piece in enumerate(split(turned, 2)):
            table[t * LANES : (t + 1) * LANES, i * hi_count : (i + 1) * hi_count] = piece

    total[...] = jnp.zeros_like(total)
    rows_each = WIDE // LANES

    def step(k, carry):
        def rows(ref):
            return jnp.concatenate(
                [ref[pl.ds(k * rows_each + i, 1), :] for i in range(rows_each)], axis=1
            )

        cells, atms, owners, weights = rows(cell), rows(atm), rows(owner), rows(weight)
        hi = place_of(owners) * blocks + (atms >> 7)
        lo = atms & (LANES - 1)
        hi_hot = (lax.broadcasted_iota(jnp.int32, (hi_count, WIDE), 0) == hi).astype(
            jnp.float32
        ).astype(jnp.bfloat16)
        picked = jnp.dot(
            table[...], jnp.concatenate([hi_hot, hi_hot], axis=0),
            preferred_element_type=jnp.float32,
        )
        lane_row = lax.broadcasted_iota(jnp.int32, (LANES, WIDE), 0)
        lo_mask = lane_row == lo
        col_hot = (lane_row == (cells & (cols - 1))).astype(jnp.float32).astype(jnp.bfloat16)
        row_mask = lax.broadcasted_iota(jnp.int32, (row_count, WIDE), 0) == (cells >> 7)
        parts = []
        for t in range(values):
            chosen = jnp.where(lo_mask, picked[t * LANES : (t + 1) * LANES, :], 0.0)
            value = jnp.sum(chosen, axis=0, keepdims=True) * weights
            parts.append(jnp.where(row_mask, value, 0.0))
        left = jnp.concatenate(parts, axis=0)
        left = jnp.concatenate(split(left, 2), axis=0)
        total[...] += lax.dot_general(
            left, col_hot, (((1,), (1,)), ((), ())), preferred_element_type=jnp.float32
        )
        return carry

    lax.fori_loop(0, cell.shape[0] // rows_each, step, 0)

    mirror[...] = from_north[...]

    @pl.when(is_top)
    def _():
        top_copy.wait()
        depth = FOLD_STEP * LANES
        lane_row = lax.broadcasted_iota(jnp.int32, (depth, LANES), 0)
        pad = mirror.shape[0]
        spot = place_of(fold[...] >> 7) * LANES + (fold[...] & (LANES - 1))

        def fold_step(k, acc):
            block = jnp.concatenate(
                [top_rows[FOLD_STEP * k + i] for i in range(FOLD_STEP)], axis=1
            )
            hot = (lane_row == spot - k * depth).astype(jnp.float32).astype(jnp.bfloat16)
            return acc + jnp.dot(
                jnp.concatenate(split(block, 2), axis=0), hot, preferred_element_type=jnp.float32
            )

        acc = lax.fori_loop(
            0, lon_count // FOLD_STEP, fold_step, jnp.zeros((2 * pad, LANES), jnp.float32)
        )
        mirror[...] = acc[:pad] + acc[pad:]

    mask = om[...].astype(jnp.float32)
    lane = lax.broadcasted_iota(jnp.int32, (row_count, cols), 1)
    row = lax.broadcasted_iota(jnp.int32, (row_count, cols), 0)
    west_cols = from_west[...]
    east_cols = from_east[...]
    south_rows = jnp.where(is_bottom, 0.0, from_south[...])

    def to_west(x, p):
        return jnp.where(lane == 0, west_cols[:, p : p + 1], pltpu.roll(x, 1, 1))

    def to_east(x, p):
        return jnp.where(lane == cols - 1, east_cols[:, p : p + 1], pltpu.roll(x, cols - 1, 1))

    def to_south(x, p):
        return jnp.where(row == 0, south_rows[p : p + 1, :], pltpu.roll(x, 1, 0))

    def to_north(x, p):
        return jnp.where(row == row_count - 1, mirror[p : p + 1, :], pltpu.roll(x, row_count - 1, 0))

    mask_at = plane_count
    open_east = mask * to_east(mask, mask_at)
    open_west = to_west(mask, mask_at) * mask
    open_north = mask * to_north(mask, mask_at)
    open_south = to_south(mask, mask_at) * mask
    pivots = []
    ratios = []
    for level in range(level_count):
        lower = mix[level] if level < level_count - 1 else jnp.zeros_like(mask)
        if level == 0:
            pivot = 1.0 + lower
        else:
            pivot = 1.0 + mix[level - 1] + lower - mix[level - 1] * ratios[-1]
        inverse = 1.0 / pivot
        pivots.append(inverse)
        ratios.append(lower * inverse)
    done = [[] for _ in range(tracer_count)]
    lines = tracer_count + 1
    half = lines * row_count
    sums = total[0:half, :] + total[half : 2 * half, :]
    last_sum = sums[tracer_count * row_count :, :]
    for level in range(level_count):
        speed_e = es[level]
        speed_w = to_west(speed_e, mask_at + 1 + level)
        speed_n = ns[level]
        speed_s = to_south(speed_n, mask_at + 1 + level)
        for t in range(tracer_count):
            p = t * level_count + level
            x = tr[t, level]
            flux_e = speed_e * jnp.where(speed_e > 0, x, to_east(x, p)) * open_east
            flux_w = speed_w * jnp.where(speed_w > 0, to_west(x, p), x) * open_west
            flux_n = speed_n * jnp.where(speed_n > 0, x, to_north(x, p)) * open_north
            flux_s = speed_s * jnp.where(speed_s > 0, to_south(x, p), x) * open_south
            value = x - (flux_e - flux_w + flux_n - flux_s)
            if level == 0:
                surface = sums[t * row_count : (t + 1) * row_count, :] - x * last_sum
                value = value + flux_step * surface
            else:
                value = value + mix[level - 1] * done[t][-1]
            done[t].append(value * pivots[level])
    for t in range(tracer_count):
        x = done[t][-1]
        out[t, level_count - 1] = x * mask
        for level in range(level_count - 2, -1, -1):
            x = done[t][level] + ratios[level] * x
            out[t, level] = x * mask


def body(
    tracers,
    east_speed,
    north_speed,
    mixing_coef,
    ocean_mask,
    fold_map,
    atmos_state,
    atmos_coef,
    xgrid_cell,
    xgrid_atm,
    xgrid_owner,
    xgrid_weight,
):
    tracer_count, level_count, row_count, cols = tracers.shape
    lon_count = lax.axis_size("lon")
    lat_count = lax.axis_size("lat")
    plane_count = tracer_count * level_count
    blocks = atmos_coef.shape[0] // LANES
    base = (tracer_count + 1) * blocks
    pad = -(-(plane_count + 1) // 8) * 8
    north_pad = -(-(plane_count + 1 + level_count) // 8) * 8
    f32 = jnp.float32
    vmem = pl.BlockSpec(memory_space=pltpu.VMEM)
    anywhere = pl.BlockSpec(memory_space=pl.ANY)
    edges = (
        jax.ShapeDtypeStruct((north_pad, cols), f32),
        jax.ShapeDtypeStruct((pad, cols), f32),
        jax.ShapeDtypeStruct((row_count, cols), f32),
        jax.ShapeDtypeStruct((row_count, cols), f32),
    )
    air, north, south, east, west = pl.pallas_call(
        pack_kernel,
        out_shape=(jax.ShapeDtypeStruct((base, cols), f32),) + edges,
        in_specs=[vmem] * 6,
        out_specs=(vmem,) * 5,
        name="pack_edges",
    )(tracers, east_speed, north_speed, ocean_mask, atmos_state, atmos_coef.reshape(blocks, LANES))
    z_count = lon_count // Y_GROUPS
    spots = (z_count, Y_GROUPS)
    air_all, top_all, from_south, from_north, from_west, from_east = pl.pallas_call(
        exchange_kernel,
        out_shape=(
            jax.ShapeDtypeStruct(spots + (base, cols), f32),
            jax.ShapeDtypeStruct(spots + (pad, cols), f32),
        ) + edges,
        in_specs=[vmem] * 5,
        out_specs=(vmem, anywhere) + (vmem,) * 4,
        scratch_shapes=[
            pltpu.SemaphoreType.DMA(spots),
            pltpu.SemaphoreType.DMA(spots),
            pltpu.SemaphoreType.DMA(spots),
            pltpu.SemaphoreType.DMA(spots),
            pltpu.SemaphoreType.DMA((4,)),
            pltpu.SemaphoreType.DMA((4,)),
            pltpu.SemaphoreType.DMA((2,)),
        ],
        compiler_params=pltpu.CompilerParams(collective_id=0, has_side_effects=True),
        name="exchange_edges",
    )(air, north, south, east, west)
    rows = xgrid_cell.shape[0] // LANES
    return pl.pallas_call(
        main_kernel,
        out_shape=jax.ShapeDtypeStruct(tracers.shape, f32),
        in_specs=[vmem] * 7 + [anywhere] + [vmem] * 8,
        out_specs=vmem,
        scratch_shapes=[
            pltpu.VMEM(((tracer_count + 1) * LANES, 2 * lon_count * blocks), jnp.bfloat16),
            pltpu.VMEM((2 * (tracer_count + 1) * row_count, cols), f32),
            pltpu.VMEM((pad, cols), f32),
            pltpu.VMEM((lon_count, pad, cols), f32),
            pltpu.SemaphoreType.DMA(()),
        ],
        name="exchange_and_solve",
    )(
        tracers, east_speed, north_speed, mixing_coef, ocean_mask, fold_map.reshape(1, cols),
        air_all.reshape(lon_count, base, cols), top_all.reshape(lon_count, pad, cols), from_south, from_north, from_west, from_east,
        xgrid_cell.reshape(rows, LANES), xgrid_atm.reshape(rows, LANES),
        xgrid_owner.reshape(rows, LANES), xgrid_weight.reshape(rows, LANES),
    )


def solution(mesh):
    in_specs = (
        P(None, None, "lat", "lon"),
        P(None, "lat", "lon"),
        P(None, "lat", "lon"),
        P(None, "lat", "lon"),
        P("lat", "lon"),
        P("lon"),
        P(None, ("lon", "lat")),
        P(("lon", "lat")),
        P(("lon", "lat")),
        P(("lon", "lat")),
        P(("lon", "lat"), None),
        P(("lon", "lat")),
    )
    out_specs = P(None, None, "lat", "lon")
    return jax.shard_map(body, mesh=mesh, in_specs=in_specs, out_specs=out_specs, check_vma=False)
```

```python
import jax
import jax.numpy as jnp
from jax import lax
from jax.experimental import pallas as pl
from jax.experimental.pallas import tpu as pltpu
from jax.sharding import PartitionSpec as P

flux_step = 0.5
LANES = 128
WIDE = 2048
FOLD_STEP = 16
Y_GROUPS = 4


def pack_edges(tr, es, ns, om, state, coef, air, north, south, east, west):
    tracer_count, level_count, row_count, cols = tr.shape
    blocks = state.shape[1] // LANES
    for t in range(tracer_count):
        for h in range(blocks):
            air[t * blocks + h : t * blocks + h + 1, :] = state[t : t + 1, h * LANES : (h + 1) * LANES]
    air[tracer_count * blocks : (tracer_count + 1) * blocks, :] = coef[...]
    plane_count = tracer_count * level_count
    lane = lax.broadcasted_iota(jnp.int32, (row_count, cols), 1)
    mask = om[...].astype(jnp.float32)
    north[...] = jnp.zeros_like(north)
    south[...] = jnp.zeros_like(south)
    first = jnp.zeros((row_count, cols), jnp.float32)
    last = jnp.zeros((row_count, cols), jnp.float32)
    for p in range(plane_count + 1 + level_count):
        if p < plane_count:
            plane = tr[p // level_count, p % level_count]
            north_plane = plane
        elif p == plane_count:
            plane = mask
            north_plane = plane
        else:
            plane = es[p - plane_count - 1]
            north_plane = ns[p - plane_count - 1]
        north[p : p + 1, :] = north_plane[row_count - 1 : row_count, :]
        last = jnp.where(lane == p, plane[:, cols - 1 : cols], last)
        if p <= plane_count:
            south[p : p + 1, :] = plane[0:1, :]
            first = jnp.where(lane == p, plane[:, 0:1], first)
    east[...] = last
    west[...] = first


def exchange_kernel(
    tr, es, ns, om, state, coef,
    air_all, top_all, from_south, from_north, from_west, from_east,
    air, north, south, east, west,
    send_air, recv_air, send_top, recv_top, send_edge, recv_edge, own,
):
    z_count = air_all.shape[0]
    lon_count = z_count * Y_GROUPS
    lat_count = lax.axis_size("lat")
    lon = lax.axis_index("lon")
    lat = lax.axis_index("lat")
    z = lax.rem(lon, z_count)
    y_base = lon - z
    z_right = {"lon": y_base + lax.rem(z + 1, z_count)}
    z_left = {"lon": y_base + lax.rem(z + z_count - 1, z_count)}
    y_to = [{"lon": lax.rem(lon + d * z_count, lon_count)} for d in range(Y_GROUPS)]
    lon_right = {"lon": lax.rem(lon + 1, lon_count)}
    lon_left = {"lon": lax.rem(lon + lon_count - 1, lon_count)}
    lat_up = {"lat": lax.rem(lat + 1, lat_count)}
    lat_down = {"lat": lax.rem(lat + lat_count - 1, lat_count)}
    partners = [z_right, z_left, lon_right, lon_left, lat_up, lat_down] + y_to[1:]
    is_top = lat == lat_count - 1
    mesh_ids = pl.DeviceIdType.MESH

    barrier = pltpu.get_barrier_semaphore()
    for partner in partners:
        pl.semaphore_signal(barrier, inc=1, device_id=partner, device_id_type=mesh_ids)
    pack_edges(tr, es, ns, om, state, coef, air, north, south, east, west)
    pl.semaphore_wait(barrier, len(partners))

    edges = []
    for i, (src, dst, target) in enumerate(
        ((north, from_south, lat_up), (south, from_north, lat_down),
         (east, from_west, lon_right), (west, from_east, lon_left))
    ):
        edges.append(
            pltpu.make_async_remote_copy(
                src_ref=src, dst_ref=dst, send_sem=send_edge.at[i], recv_sem=recv_edge.at[i],
                device_id=target, device_id_type=mesh_ids,
            )
        )

    right_steps = z_count // 2
    left_steps = z_count - 1 - right_steps
    pad = top_all.shape[2]

    def flow(first, slots, send, recv):
        def copy(slot, d):
            if slot == 0:
                src, dst, target = first, slots.at[0, d], y_to[d]
            else:
                if slot <= right_steps:
                    before, target = slot - 1, z_right
                else:
                    before, target = (slot + 1) % z_count, z_left
                if d == 0:
                    src = first if before == 0 else slots.at[before, 0]
                    dst = slots.at[slot, 0]
                else:
                    src = slots.at[before, 1:Y_GROUPS]
                    dst = slots.at[slot, 1:Y_GROUPS]
            return pltpu.make_async_remote_copy(
                src_ref=src, dst_ref=dst, send_sem=send.at[slot, d],
                recv_sem=recv.at[slot, d], device_id=target, device_id_type=mesh_ids,
            )

        return copy

    air_flow = flow(air, air_all, send_air, recv_air)
    top_flow = flow(north.at[0:pad], top_all, send_top, recv_top)
    air_own = pltpu.make_async_copy(air, air_all.at[0, 0], own.at[0])
    top_own = pltpu.make_async_copy(north.at[0:pad], top_all.at[0, 0], own.at[1])

    def begin(copy):
        for d in range(1, Y_GROUPS):
            copy(0, d).start()
        copy(1, 0).start()
        copy(z_count - 1, 0).start()

    def advance(copy, step, d):
        if step == 0:
            if d:
                for group in range(1, Y_GROUPS):
                    copy(0, group).wait_recv()
                copy(1, 1).start()
                copy(z_count - 1, 1).start()
            return
        copy(step, d).wait_recv()
        if step < right_steps:
            copy(step + 1, d).start()
        if step <= left_steps:
            copy(z_count - step, d).wait_recv()
            if step < left_steps:
                copy(z_count - step - 1, d).start()

    order = []
    for d in (0, 1):
        delay = 1.5 * d
        for step in range(right_steps + 1):
            order.append((step + delay, d, step, False))
            order.append((step + delay + 0.6, d, step, True))
    order.sort()

    def finish(copy):
        for group in range(1, Y_GROUPS):
            copy(0, group).wait_send()
        for slot in range(1, z_count):
            copy(slot, 0).wait_send()
            copy(slot, 1).wait_send()

    for edge in edges:
        edge.start()
    begin(air_flow)
    air_own.start()

    @pl.when(is_top)
    def _():
        begin(top_flow)
        top_own.start()

    for _, d, step, is_fold in order:
        if is_fold:

            @pl.when(is_top)
            def _():
                advance(top_flow, step, d)

        else:
            advance(air_flow, step, d)

    finish(air_flow)
    air_own.wait()

    @pl.when(is_top)
    def _():
        finish(top_flow)
        top_own.wait()

    for edge in edges:
        edge.wait()


def split(x, pieces):
    out = []
    for i in range(pieces):
        top = x.astype(jnp.bfloat16)
        out.append(top)
        x = x - top.astype(jnp.float32)
    return out


def main_kernel(
    tr, es, ns, mix, om, fold, gat, top_all, from_south, from_north, from_west, from_east,
    cell, atm, owner, weight, out, table, total, mirror, top_rows, top_sem,
):
    tracer_count, level_count, row_count, cols = tr.shape
    lon_count = gat.shape[0]
    values = tracer_count + 1
    blocks = 1024 // LANES
    base = values * blocks
    hi_count = lon_count * blocks
    z_count = lon_count // Y_GROUPS
    lon = lax.axis_index("lon")
    my_z = lax.rem(lon, z_count)
    my_y = lax.div(lon, z_count)
    plane_count = tracer_count * level_count
    lat_count = lax.axis_size("lat")
    is_top = lax.axis_index("lat") == lat_count - 1
    is_bottom = lax.axis_index("lat") == 0

    top_copy = pltpu.make_async_copy(top_all, top_rows, top_sem)

    @pl.when(is_top)
    def _():
        top_copy.start()

    def place_of(owners):
        y = jnp.zeros_like(owners)
        for group in range(1, Y_GROUPS):
            y = y + (owners >= group * z_count).astype(jnp.int32)
        far_z = my_z - (owners - y * z_count)
        far_y = my_y - y
        far_z = jnp.where(far_z < 0, far_z + z_count, far_z)
        far_y = jnp.where(far_y < 0, far_y + Y_GROUPS, far_y)
        return far_z * Y_GROUPS + far_y

    coef = gat[:, tracer_count * blocks : base, :].reshape(hi_count, LANES)
    for t in range(values):
        if t < tracer_count:
            block = gat[:, t * blocks : (t + 1) * blocks, :].reshape(hi_count, LANES) * coef
        else:
            block = coef
        turned = block.T
        for i, piece in enumerate(split(turned, 2)):
            table[t * LANES : (t + 1) * LANES, i * hi_count : (i + 1) * hi_count] = piece

    total[...] = jnp.zeros_like(total)
    rows_each = WIDE // LANES

    def step(k, carry):
        def rows(ref):
            return jnp.concatenate(
                [ref[pl.ds(k * rows_each + i, 1), :] for i in range(rows_each)], axis=1
            )

        cells, atms, owners, weights = rows(cell), rows(atm), rows(owner), rows(weight)
        hi = place_of(owners) * blocks + (atms >> 7)
        lo = atms & (LANES - 1)
        hi_hot = (lax.broadcasted_iota(jnp.int32, (hi_count, WIDE), 0) == hi).astype(
            jnp.float32
        ).astype(jnp.bfloat16)
        picked = jnp.dot(
            table[...], jnp.concatenate([hi_hot, hi_hot], axis=0),
            preferred_element_type=jnp.float32,
        )
        lane_row = lax.broadcasted_iota(jnp.int32, (LANES, WIDE), 0)
        lo_mask = lane_row == lo
        col_hot = (lane_row == (cells & (cols - 1))).astype(jnp.float32).astype(jnp.bfloat16)
        row_mask = lax.broadcasted_iota(jnp.int32, (row_count, WIDE), 0) == (cells >> 7)
        parts = []
        for t in range(values):
            chosen = jnp.where(lo_mask, picked[t * LANES : (t + 1) * LANES, :], 0.0)
            value = jnp.sum(chosen, axis=0, keepdims=True) * weights
            parts.append(jnp.where(row_mask, value, 0.0))
        left = jnp.concatenate(parts, axis=0)
        left = jnp.concatenate(split(left, 2), axis=0)
        total[...] += lax.dot_general(
            left, col_hot, (((1,), (1,)), ((), ())), preferred_element_type=jnp.float32
        )
        return carry

    lax.fori_loop(0, cell.shape[0] // rows_each, step, 0)

    mirror[...] = from_north[...]

    @pl.when(is_top)
    def _():
        top_copy.wait()
        depth = FOLD_STEP * LANES
        lane_row = lax.broadcasted_iota(jnp.int32, (depth, LANES), 0)
        pad = mirror.shape[0]
        spot = place_of(fold[...] >> 7) * LANES + (fold[...] & (LANES - 1))

        def fold_step(k, acc):
            block = jnp.concatenate(
                [top_rows[FOLD_STEP * k + i] for i in range(FOLD_STEP)], axis=1
            )
            hot = (lane_row == spot - k * depth).astype(jnp.float32).astype(jnp.bfloat16)
            return acc + jnp.dot(
                jnp.concatenate(split(block, 2), axis=0), hot, preferred_element_type=jnp.float32
            )

        acc = lax.fori_loop(
            0, lon_count // FOLD_STEP, fold_step, jnp.zeros((2 * pad, LANES), jnp.float32)
        )
        mirror[...] = acc[:pad] + acc[pad:]

    mask = om[...].astype(jnp.float32)
    lane = lax.broadcasted_iota(jnp.int32, (row_count, cols), 1)
    row = lax.broadcasted_iota(jnp.int32, (row_count, cols), 0)
    west_cols = from_west[...]
    east_cols = from_east[...]
    south_rows = jnp.where(is_bottom, 0.0, from_south[...])

    def to_west(x, p):
        return jnp.where(lane == 0, west_cols[:, p : p + 1], pltpu.roll(x, 1, 1))

    def to_east(x, p):
        return jnp.where(lane == cols - 1, east_cols[:, p : p + 1], pltpu.roll(x, cols - 1, 1))

    def to_south(x, p):
        return jnp.where(row == 0, south_rows[p : p + 1, :], pltpu.roll(x, 1, 0))

    def to_north(x, p):
        return jnp.where(row == row_count - 1, mirror[p : p + 1, :], pltpu.roll(x, row_count - 1, 0))

    mask_at = plane_count
    open_east = mask * to_east(mask, mask_at)
    open_west = to_west(mask, mask_at) * mask
    open_north = mask * to_north(mask, mask_at)
    open_south = to_south(mask, mask_at) * mask
    pivots = []
    ratios = []
    for level in range(level_count):
        lower = mix[level] if level < level_count - 1 else jnp.zeros_like(mask)
        if level == 0:
            pivot = 1.0 + lower
        else:
            pivot = 1.0 + mix[level - 1] + lower - mix[level - 1] * ratios[-1]
        inverse = 1.0 / pivot
        pivots.append(inverse)
        ratios.append(lower * inverse)
    done = [[] for _ in range(tracer_count)]
    lines = tracer_count + 1
    half = lines * row_count
    sums = total[0:half, :] + total[half : 2 * half, :]
    last_sum = sums[tracer_count * row_count :, :]
    for level in range(level_count):
        speed_e = es[level]
        speed_w = to_west(speed_e, mask_at + 1 + level)
        speed_n = ns[level]
        speed_s = to_south(speed_n, mask_at + 1 + level)
        for t in range(tracer_count):
            p = t * level_count + level
            x = tr[t, level]
            flux_e = speed_e * jnp.where(speed_e > 0, x, to_east(x, p)) * open_east
            flux_w = speed_w * jnp.where(speed_w > 0, to_west(x, p), x) * open_west
            flux_n = speed_n * jnp.where(speed_n > 0, x, to_north(x, p)) * open_north
            flux_s = speed_s * jnp.where(speed_s > 0, to_south(x, p), x) * open_south
            value = x - (flux_e - flux_w + flux_n - flux_s)
            if level == 0:
                surface = sums[t * row_count : (t + 1) * row_count, :] - x * last_sum
                value = value + flux_step * surface
            else:
                value = value + mix[level - 1] * done[t][-1]
            done[t].append(value * pivots[level])
    for t in range(tracer_count):
        x = done[t][-1]
        out[t, level_count - 1] = x * mask
        for level in range(level_count - 2, -1, -1):
            x = done[t][level] + ratios[level] * x
            out[t, level] = x * mask


def body(
    tracers,
    east_speed,
    north_speed,
    mixing_coef,
    ocean_mask,
    fold_map,
    atmos_state,
    atmos_coef,
    xgrid_cell,
    xgrid_atm,
    xgrid_owner,
    xgrid_weight,
):
    tracer_count, level_count, row_count, cols = tracers.shape
    lon_count = lax.axis_size("lon")
    lat_count = lax.axis_size("lat")
    plane_count = tracer_count * level_count
    blocks = atmos_coef.shape[0] // LANES
    base = (tracer_count + 1) * blocks
    pad = -(-(plane_count + 1) // 8) * 8
    north_pad = -(-(plane_count + 1 + level_count) // 8) * 8
    f32 = jnp.float32
    vmem = pl.BlockSpec(memory_space=pltpu.VMEM)
    anywhere = pl.BlockSpec(memory_space=pl.ANY)
    edges = (
        jax.ShapeDtypeStruct((north_pad, cols), f32),
        jax.ShapeDtypeStruct((pad, cols), f32),
        jax.ShapeDtypeStruct((row_count, cols), f32),
        jax.ShapeDtypeStruct((row_count, cols), f32),
    )
    z_count = lon_count // Y_GROUPS
    spots = (z_count, Y_GROUPS)
    air_all, top_all, from_south, from_north, from_west, from_east = pl.pallas_call(
        exchange_kernel,
        out_shape=(
            pltpu.VMEM(spots + (base, cols), f32),
            jax.ShapeDtypeStruct(spots + (pad, cols), f32),
        ) + edges,
        in_specs=[vmem] * 6,
        out_specs=(vmem, anywhere) + (vmem,) * 4,
        scratch_shapes=[
            pltpu.VMEM((base, cols), f32),
            pltpu.VMEM((north_pad, cols), f32),
            pltpu.VMEM((pad, cols), f32),
            pltpu.VMEM((row_count, cols), f32),
            pltpu.VMEM((row_count, cols), f32),
            pltpu.SemaphoreType.DMA(spots),
            pltpu.SemaphoreType.DMA(spots),
            pltpu.SemaphoreType.DMA(spots),
            pltpu.SemaphoreType.DMA(spots),
            pltpu.SemaphoreType.DMA((4,)),
            pltpu.SemaphoreType.DMA((4,)),
            pltpu.SemaphoreType.DMA((2,)),
        ],
        compiler_params=pltpu.CompilerParams(collective_id=0, has_side_effects=True),
        name="exchange_edges",
    )(tracers, east_speed, north_speed, ocean_mask, atmos_state, atmos_coef.reshape(blocks, LANES))
    rows = xgrid_cell.shape[0] // LANES
    return pl.pallas_call(
        main_kernel,
        out_shape=jax.ShapeDtypeStruct(tracers.shape, f32),
        in_specs=[vmem] * 7 + [anywhere] + [vmem] * 8,
        out_specs=vmem,
        scratch_shapes=[
            pltpu.VMEM(((tracer_count + 1) * LANES, 2 * lon_count * blocks), jnp.bfloat16),
            pltpu.VMEM((2 * (tracer_count + 1) * row_count, cols), f32),
            pltpu.VMEM((pad, cols), f32),
            pltpu.VMEM((lon_count, pad, cols), f32),
            pltpu.SemaphoreType.DMA(()),
        ],
        name="exchange_and_solve",
    )(
        tracers, east_speed, north_speed, mixing_coef, ocean_mask, fold_map.reshape(1, cols),
        air_all.reshape(lon_count, base, cols), top_all.reshape(lon_count, pad, cols), from_south, from_north, from_west, from_east,
        xgrid_cell.reshape(rows, LANES), xgrid_atm.reshape(rows, LANES),
        xgrid_owner.reshape(rows, LANES), xgrid_weight.reshape(rows, LANES),
    )


def solution(mesh):
    in_specs = (
        P(None, None, "lat", "lon"),
        P(None, "lat", "lon"),
        P(None, "lat", "lon"),
        P(None, "lat", "lon"),
        P("lat", "lon"),
        P("lon"),
        P(None, ("lon", "lat")),
        P(("lon", "lat")),
        P(("lon", "lat")),
        P(("lon", "lat")),
        P(("lon", "lat"), None),
        P(("lon", "lat")),
    )
    out_specs = P(None, None, "lat", "lon")
    return jax.shard_map(body, mesh=mesh, in_specs=in_specs, out_specs=out_specs, check_vma=False)
```

```python
import jax
import jax.numpy as jnp
from jax import lax
from jax.experimental import pallas as pl
from jax.experimental.pallas import tpu as pltpu
from jax.sharding import PartitionSpec as P

flux_step = 0.5
LANES = 128
WIDE = 2048
FOLD_STEP = 16
Y_GROUPS = 4


def pack_edges(tr, es, ns, om, state, coef, air, north, south, east, west):
    tracer_count, level_count, row_count, cols = tr.shape
    blocks = state.shape[1] // LANES
    for t in range(tracer_count):
        for h in range(blocks):
            air[t * blocks + h : t * blocks + h + 1, :] = state[t : t + 1, h * LANES : (h + 1) * LANES]
    air[tracer_count * blocks : (tracer_count + 1) * blocks, :] = coef[...]
    plane_count = tracer_count * level_count
    lane = lax.broadcasted_iota(jnp.int32, (row_count, cols), 1)
    mask = om[...].astype(jnp.float32)
    north[...] = jnp.zeros_like(north)
    south[...] = jnp.zeros_like(south)
    first = jnp.zeros((row_count, cols), jnp.float32)
    last = jnp.zeros((row_count, cols), jnp.float32)
    for p in range(plane_count + 1 + level_count):
        if p < plane_count:
            plane = tr[p // level_count, p % level_count]
            north_plane = plane
        elif p == plane_count:
            plane = mask
            north_plane = plane
        else:
            plane = es[p - plane_count - 1]
            north_plane = ns[p - plane_count - 1]
        north[p : p + 1, :] = north_plane[row_count - 1 : row_count, :]
        last = jnp.where(lane == p, plane[:, cols - 1 : cols], last)
        if p <= plane_count:
            south[p : p + 1, :] = plane[0:1, :]
            first = jnp.where(lane == p, plane[:, 0:1], first)
    east[...] = last
    west[...] = first


def exchange_kernel(
    tr, es, ns, om, state, coef,
    air_all, top_all, from_south, from_north, from_west, from_east,
    air, north, south, east, west,
    send_air, recv_air, send_top, recv_top, send_edge, recv_edge, own,
):
    z_count = air_all.shape[0]
    lon_count = z_count * Y_GROUPS
    lat_count = lax.axis_size("lat")
    lon = lax.axis_index("lon")
    lat = lax.axis_index("lat")
    z = lax.rem(lon, z_count)
    y_base = lon - z
    z_right = {"lon": y_base + lax.rem(z + 1, z_count)}
    z_left = {"lon": y_base + lax.rem(z + z_count - 1, z_count)}
    y_to = [{"lon": lax.rem(lon + d * z_count, lon_count)} for d in range(Y_GROUPS)]
    lon_right = {"lon": lax.rem(lon + 1, lon_count)}
    lon_left = {"lon": lax.rem(lon + lon_count - 1, lon_count)}
    lat_up = {"lat": lax.rem(lat + 1, lat_count)}
    lat_down = {"lat": lax.rem(lat + lat_count - 1, lat_count)}
    partners = [z_right, z_left, lon_right, lon_left, lat_up, lat_down] + y_to[1:]
    is_top = lat == lat_count - 1
    mesh_ids = pl.DeviceIdType.MESH

    barrier = pltpu.get_barrier_semaphore()
    for partner in partners:
        pl.semaphore_signal(barrier, inc=1, device_id=partner, device_id_type=mesh_ids)
    pack_edges(tr, es, ns, om, state, coef, air, north, south, east, west)
    pl.semaphore_wait(barrier, len(partners))

    edges = []
    for i, (src, dst, target) in enumerate(
        ((north, from_south, lat_up), (south, from_north, lat_down),
         (east, from_west, lon_right), (west, from_east, lon_left))
    ):
        edges.append(
            pltpu.make_async_remote_copy(
                src_ref=src, dst_ref=dst, send_sem=send_edge.at[i], recv_sem=recv_edge.at[i],
                device_id=target, device_id_type=mesh_ids,
            )
        )

    right_steps = z_count // 2
    left_steps = z_count - 1 - right_steps
    pad = top_all.shape[2]

    def flow(first, slots, send, recv):
        def copy(slot, d):
            if slot == 0:
                src, dst, target = first, slots.at[0, d], y_to[d]
            else:
                if slot <= right_steps:
                    before, target = slot - 1, z_right
                else:
                    before, target = (slot + 1) % z_count, z_left
                if d == 0:
                    src = first if before == 0 else slots.at[before, 0]
                    dst = slots.at[slot, 0]
                else:
                    src = slots.at[before, 1:Y_GROUPS]
                    dst = slots.at[slot, 1:Y_GROUPS]
            return pltpu.make_async_remote_copy(
                src_ref=src, dst_ref=dst, send_sem=send.at[slot, d],
                recv_sem=recv.at[slot, d], device_id=target, device_id_type=mesh_ids,
            )

        return copy

    air_flow = flow(air, air_all, send_air, recv_air)
    top_flow = flow(north.at[0:pad], top_all, send_top, recv_top)
    air_own = pltpu.make_async_copy(air, air_all.at[0, 0], own.at[0])
    top_own = pltpu.make_async_copy(north.at[0:pad], top_all.at[0, 0], own.at[1])

    def begin(copy):
        for d in range(1, Y_GROUPS):
            copy(0, d).start()
        copy(1, 0).start()
        copy(z_count - 1, 0).start()

    def advance(copy, step, d):
        if step == 0:
            if d:
                for group in range(1, Y_GROUPS):
                    copy(0, group).wait_recv()
                copy(1, 1).start()
                copy(z_count - 1, 1).start()
            return
        copy(step, d).wait_recv()
        if step < right_steps:
            copy(step + 1, d).start()
        if step <= left_steps:
            copy(z_count - step, d).wait_recv()
            if step < left_steps:
                copy(z_count - step - 1, d).start()

    order = []
    for d in (0, 1):
        delay = 1.5 * d
        for step in range(right_steps + 1):
            order.append((step + delay, d, step, False))
            order.append((step + delay + 0.6, d, step, True))
    order.sort()

    def finish(copy):
        for group in range(1, Y_GROUPS):
            copy(0, group).wait_send()
        for slot in range(1, z_count):
            copy(slot, 0).wait_send()
            copy(slot, 1).wait_send()

    for edge in edges:
        edge.start()
    begin(air_flow)
    air_own.start()

    @pl.when(is_top)
    def _():
        begin(top_flow)
        top_own.start()

    for _, d, step, is_fold in order:
        if is_fold:

            @pl.when(is_top)
            def _():
                advance(top_flow, step, d)

        else:
            advance(air_flow, step, d)

    finish(air_flow)
    air_own.wait()

    @pl.when(is_top)
    def _():
        finish(top_flow)
        top_own.wait()

    for edge in edges:
        edge.wait()


def split(x, pieces):
    out = []
    for i in range(pieces):
        top = x.astype(jnp.bfloat16)
        out.append(top)
        x = x - top.astype(jnp.float32)
    return out


def main_kernel(
    tr, es, ns, mix, om, fold, gat, top_all, from_south, from_north, from_west, from_east,
    cell, atm, owner, weight, out, table, total, mirror, top_rows, top_sem,
):
    tracer_count, level_count, row_count, cols = tr.shape
    lon_count = gat.shape[0]
    values = tracer_count + 1
    blocks = 1024 // LANES
    base = values * blocks
    hi_count = lon_count * blocks
    z_count = lon_count // Y_GROUPS
    lon = lax.axis_index("lon")
    my_z = lax.rem(lon, z_count)
    my_y = lax.div(lon, z_count)
    plane_count = tracer_count * level_count
    lat_count = lax.axis_size("lat")
    is_top = lax.axis_index("lat") == lat_count - 1
    is_bottom = lax.axis_index("lat") == 0

    top_copy = pltpu.make_async_copy(top_all, top_rows, top_sem)

    @pl.when(is_top)
    def _():
        top_copy.start()

    def place_of(owners):
        y = jnp.zeros_like(owners)
        for group in range(1, Y_GROUPS):
            y = y + (owners >= group * z_count).astype(jnp.int32)
        far_z = my_z - (owners - y * z_count)
        far_y = my_y - y
        far_z = jnp.where(far_z < 0, far_z + z_count, far_z)
        far_y = jnp.where(far_y < 0, far_y + Y_GROUPS, far_y)
        return far_z * Y_GROUPS + far_y

    coef = gat[:, tracer_count * blocks : base, :].reshape(hi_count, LANES)
    for t in range(values):
        if t < tracer_count:
            block = gat[:, t * blocks : (t + 1) * blocks, :].reshape(hi_count, LANES) * coef
        else:
            block = coef
        turned = block.T
        for i, piece in enumerate(split(turned, 2)):
            table[t * LANES : (t + 1) * LANES, i * hi_count : (i + 1) * hi_count] = piece

    total[...] = jnp.zeros_like(total)
    rows_each = WIDE // LANES

    def step(k, carry):
        def rows(ref):
            return jnp.concatenate(
                [ref[pl.ds(k * rows_each + i, 1), :] for i in range(rows_each)], axis=1
            )

        cells, atms, owners, weights = rows(cell), rows(atm), rows(owner), rows(weight)
        hi = place_of(owners) * blocks + (atms >> 7)
        lo = atms & (LANES - 1)
        hi_hot = (lax.broadcasted_iota(jnp.int32, (hi_count, WIDE), 0) == hi).astype(
            jnp.float32
        ).astype(jnp.bfloat16)
        picked = jnp.dot(
            table[...], jnp.concatenate([hi_hot, hi_hot], axis=0),
            preferred_element_type=jnp.float32,
        )
        lane_row = lax.broadcasted_iota(jnp.int32, (LANES, WIDE), 0)
        lo_mask = lane_row == lo
        col_hot = (lane_row == (cells & (cols - 1))).astype(jnp.float32).astype(jnp.bfloat16)
        row_mask = lax.broadcasted_iota(jnp.int32, (row_count, WIDE), 0) == (cells >> 7)
        parts = []
        for t in range(values):
            chosen = jnp.where(lo_mask, picked[t * LANES : (t + 1) * LANES, :], 0.0)
            value = jnp.sum(chosen, axis=0, keepdims=True) * weights
            parts.append(jnp.where(row_mask, value, 0.0))
        left = jnp.concatenate(parts, axis=0)
        left = jnp.concatenate(split(left, 2), axis=0)
        total[...] += lax.dot_general(
            left, col_hot, (((1,), (1,)), ((), ())), preferred_element_type=jnp.float32
        )
        return carry

    lax.fori_loop(0, cell.shape[0] // rows_each, step, 0)

    mirror[...] = from_north[...]

    @pl.when(is_top)
    def _():
        top_copy.wait()
        depth = FOLD_STEP * LANES
        lane_row = lax.broadcasted_iota(jnp.int32, (depth, LANES), 0)
        pad = mirror.shape[0]
        spot = place_of(fold[...] >> 7) * LANES + (fold[...] & (LANES - 1))

        def fold_step(k, acc):
            block = jnp.concatenate(
                [top_rows[FOLD_STEP * k + i] for i in range(FOLD_STEP)], axis=1
            )
            hot = (lane_row == spot - k * depth).astype(jnp.float32).astype(jnp.bfloat16)
            return acc + jnp.dot(
                jnp.concatenate(split(block, 2), axis=0), hot, preferred_element_type=jnp.float32
            )

        acc = lax.fori_loop(
            0, lon_count // FOLD_STEP, fold_step, jnp.zeros((2 * pad, LANES), jnp.float32)
        )
        mirror[...] = acc[:pad] + acc[pad:]

    mask = om[...].astype(jnp.float32)
    lane = lax.broadcasted_iota(jnp.int32, (row_count, cols), 1)
    row = lax.broadcasted_iota(jnp.int32, (row_count, cols), 0)
    west_cols = from_west[...]
    east_cols = from_east[...]
    south_rows = jnp.where(is_bottom, 0.0, from_south[...])

    def to_west(x, p):
        return jnp.where(lane == 0, west_cols[:, p : p + 1], pltpu.roll(x, 1, 1))

    def to_east(x, p):
        return jnp.where(lane == cols - 1, east_cols[:, p : p + 1], pltpu.roll(x, cols - 1, 1))

    def to_south(x, p):
        return jnp.where(row == 0, south_rows[p : p + 1, :], pltpu.roll(x, 1, 0))

    def to_north(x, p):
        return jnp.where(row == row_count - 1, mirror[p : p + 1, :], pltpu.roll(x, row_count - 1, 0))

    mask_at = plane_count
    open_east = mask * to_east(mask, mask_at)
    open_west = to_west(mask, mask_at) * mask
    open_north = mask * to_north(mask, mask_at)
    open_south = to_south(mask, mask_at) * mask
    pivots = []
    ratios = []
    for level in range(level_count):
        lower = mix[level] if level < level_count - 1 else jnp.zeros_like(mask)
        if level == 0:
            pivot = 1.0 + lower
        else:
            pivot = 1.0 + mix[level - 1] + lower - mix[level - 1] * ratios[-1]
        inverse = 1.0 / pivot
        pivots.append(inverse)
        ratios.append(lower * inverse)
    done = [[] for _ in range(tracer_count)]
    lines = tracer_count + 1
    half = lines * row_count
    sums = total[0:half, :] + total[half : 2 * half, :]
    last_sum = sums[tracer_count * row_count :, :]
    for level in range(level_count):
        speed_e = es[level]
        speed_w = to_west(speed_e, mask_at + 1 + level)
        speed_n = ns[level]
        speed_s = to_south(speed_n, mask_at + 1 + level)
        for t in range(tracer_count):
            p = t * level_count + level
            x = tr[t, level]
            flux_e = speed_e * jnp.where(speed_e > 0, x, to_east(x, p)) * open_east
            flux_w = speed_w * jnp.where(speed_w > 0, to_west(x, p), x) * open_west
            flux_n = speed_n * jnp.where(speed_n > 0, x, to_north(x, p)) * open_north
            flux_s = speed_s * jnp.where(speed_s > 0, to_south(x, p), x) * open_south
            value = x - (flux_e - flux_w + flux_n - flux_s)
            if level == 0:
                surface = sums[t * row_count : (t + 1) * row_count, :] - x * last_sum
                value = value + flux_step * surface
            else:
                value = value + mix[level - 1] * done[t][-1]
            done[t].append(value * pivots[level])
    for t in range(tracer_count):
        x = done[t][-1]
        out[t, level_count - 1] = x * mask
        for level in range(level_count - 2, -1, -1):
            x = done[t][level] + ratios[level] * x
            out[t, level] = x * mask


def body(
    tracers,
    east_speed,
    north_speed,
    mixing_coef,
    ocean_mask,
    fold_map,
    atmos_state,
    atmos_coef,
    xgrid_cell,
    xgrid_atm,
    xgrid_owner,
    xgrid_weight,
):
    tracer_count, level_count, row_count, cols = tracers.shape
    lon_count = lax.axis_size("lon")
    lat_count = lax.axis_size("lat")
    plane_count = tracer_count * level_count
    blocks = atmos_coef.shape[0] // LANES
    base = (tracer_count + 1) * blocks
    pad = -(-(plane_count + 1) // 8) * 8
    north_pad = -(-(plane_count + 1 + level_count) // 8) * 8
    f32 = jnp.float32
    vmem = pl.BlockSpec(memory_space=pltpu.VMEM)
    anywhere = pl.BlockSpec(memory_space=pl.ANY)
    edges = (
        jax.ShapeDtypeStruct((north_pad, cols), f32),
        jax.ShapeDtypeStruct((pad, cols), f32),
        jax.ShapeDtypeStruct((row_count, cols), f32),
        jax.ShapeDtypeStruct((row_count, cols), f32),
    )
    z_count = lon_count // Y_GROUPS
    spots = (z_count, Y_GROUPS)
    air_all, top_all, from_south, from_north, from_west, from_east = pl.pallas_call(
        exchange_kernel,
        out_shape=(
            pltpu.VMEM(spots + (base, cols), f32),
            jax.ShapeDtypeStruct(spots + (pad, cols), f32),
        ) + edges,
        in_specs=[vmem] * 6,
        out_specs=(vmem, anywhere) + (vmem,) * 4,
        scratch_shapes=[
            pltpu.VMEM((base, cols), f32),
            pltpu.VMEM((north_pad, cols), f32),
            pltpu.VMEM((pad, cols), f32),
            pltpu.VMEM((row_count, cols), f32),
            pltpu.VMEM((row_count, cols), f32),
            pltpu.SemaphoreType.DMA(spots),
            pltpu.SemaphoreType.DMA(spots),
            pltpu.SemaphoreType.DMA(spots),
            pltpu.SemaphoreType.DMA(spots),
            pltpu.SemaphoreType.DMA((4,)),
            pltpu.SemaphoreType.DMA((4,)),
            pltpu.SemaphoreType.DMA((2,)),
        ],
        compiler_params=pltpu.CompilerParams(collective_id=0, has_side_effects=True),
        name="exchange_edges",
    )(tracers, east_speed, north_speed, ocean_mask, atmos_state, atmos_coef.reshape(blocks, LANES))
    rows = xgrid_cell.shape[0] // LANES
    return pl.pallas_call(
        main_kernel,
        out_shape=jax.ShapeDtypeStruct(tracers.shape, f32),
        in_specs=[vmem] * 7 + [anywhere] + [vmem] * 8,
        out_specs=vmem,
        scratch_shapes=[
            pltpu.VMEM(((tracer_count + 1) * LANES, 2 * lon_count * blocks), jnp.bfloat16),
            pltpu.VMEM((2 * (tracer_count + 1) * row_count, cols), f32),
            pltpu.VMEM((pad, cols), f32),
            pltpu.VMEM((lon_count, pad, cols), f32),
            pltpu.SemaphoreType.DMA(()),
        ],
        name="exchange_and_solve",
    )(
        tracers, east_speed, north_speed, mixing_coef, ocean_mask, fold_map.reshape(1, cols),
        pltpu.with_memory_space_constraint(air_all.reshape(lon_count, base, cols), pltpu.VMEM),
        top_all.reshape(lon_count, pad, cols), from_south, from_north, from_west, from_east,
        xgrid_cell.reshape(rows, LANES), xgrid_atm.reshape(rows, LANES),
        xgrid_owner.reshape(rows, LANES), xgrid_weight.reshape(rows, LANES),
    )


def solution(mesh):
    in_specs = (
        P(None, None, "lat", "lon"),
        P(None, "lat", "lon"),
        P(None, "lat", "lon"),
        P(None, "lat", "lon"),
        P("lat", "lon"),
        P("lon"),
        P(None, ("lon", "lat")),
        P(("lon", "lat")),
        P(("lon", "lat")),
        P(("lon", "lat")),
        P(("lon", "lat"), None),
        P(("lon", "lat")),
    )
    out_specs = P(None, None, "lat", "lon")
    return jax.shard_map(body, mesh=mesh, in_specs=in_specs, out_specs=out_specs, check_vma=False)
```
